32 devices in a mesh: lat: 4 (over z), lon: 8 (over y, x, core).
Axes of the slice: x: 2, y: 2, z: 4, core: 2. Of those that a mesh axis runs over, the one named last changes fastest.
Arguments:
- state_grid: bfloat16 [24, 672, 192], P('lat', 'lon'), may hold values from -6 to 6
- norm_gain: float32 [192], replicated, may hold values from 0.1 to 1.9
- w_qkv: bfloat16 [192, 576], replicated, may hold values from -0.4375 to 0.4375
- w_proj: bfloat16 [192, 192], replicated, may hold values from -1.25 to 1.25
- bias_table: float32 [8, 6, 253], replicated, may hold values from -6 to 300
- window_kind: int32 [4, 56], replicated, may hold values from 0 to 7
- cotangent: bfloat16 [24, 672, 192], P('lat', 'lon'), may hold values from -6 to 6
Outputs:
- out_field: bfloat16 [24, 672, 192], P('lat', 'lon')
- d_field: bfloat16 [24, 672, 192], P('lat', 'lon')
- qkv_grad: float32 [192, 576], replicated
- proj_grad: float32 [192, 192], replicated
- table_grad: float32 [8, 6, 253], replicated
- gain_grad: float32 [192], replicated
The draws below stay inside these ranges and needn't reach their ends.
All inputs are finite; a program needn't handle non-finite values.
Results may differ from the reference program's by a relative error of at most 0.009.
Values may be sent and summed in bfloat16 or wider, within the bound.
A program may use at most 64 MiB of HBM per device.

```python
import jax
import jax.numpy as jnp
from jax import lax

D = 192
HEADS = 6
WIN_LAT = 6
WIN_LON = 12
KINDS = 8
NLAT = 24
NLON = 672
BANDS = 4
SECTORS = 56
REL = 253


def draw_bias_table(key, part):
    ground_key = jax.random.fold_in(key, 11)
    dims_all = (KINDS, HEADS, REL)
    return jnp.clip(jax.random.normal(ground_key, dims_all, jnp.float32), -6.0, 6.0)


def touch_ends(drawn, stream_key, least, largest):
    longest = drawn.shape.index(max(drawn.shape))
    spots = []
    for shift in (0, 1):
        where = [jax.random.randint(jax.random.fold_in(stream_key, axis), (), 0, length) for axis, length in enumerate(drawn.shape)]
        where[longest] = (where[longest] + shift) % drawn.shape[longest]
        spots.append(tuple(where))
    return drawn.at[spots[0]].set(least).at[spots[1]].set(largest)


def level_of(key, shape, split, least, high):
    level = 1.0
    for dim, parts in split:
        steps = jax.random.uniform(jax.random.fold_in(jax.random.fold_in(key, 6), dim), (parts,), jnp.float32, least / len(split), high / len(split))
        level = level * jnp.repeat(jnp.exp(steps), shape[dim] // parts).reshape((-1,) + (1,) * (len(shape) - 1 - dim))
    return level


def normal_values(key, shape, deviation, bound, cuts=(), held_as=jnp.bfloat16):
    array = deviation * jax.random.normal(key, shape, jnp.float32)
    if cuts:
        array = array * level_of(key, shape, cuts, -0.22, 0.18)
    return jnp.clip(array, -bound, bound).astype(held_as)


def setup_inputs(seed: int = 0) -> dict:
    arg_keys = jax.random.split(jax.random.key(seed), 8)
    return {
        "state_grid": normal_values(arg_keys[0], (NLAT, NLON, D), 1.0, 6.0, ((0, 4), (1, 8))),
        "norm_gain": jnp.clip(1.0 + 0.18 * jax.random.normal(arg_keys[1], (D,), jnp.float32), 0.1, 1.9),
        "w_qkv": normal_values(arg_keys[2], (D, 3 * D), D ** -0.5, 0.4375),
        "w_proj": normal_values(arg_keys[3], (D, D), (D // 8) ** -0.5, 1.25),
        "bias_table": draw_bias_table(jax.random.fold_in(arg_keys[7], 71), 0),
        "window_kind": touch_ends(jax.random.randint(arg_keys[5], (BANDS, SECTORS), 0, KINDS), jax.random.fold_in(arg_keys[5], 1), 0, KINDS - 1).astype(jnp.int32),
        "cotangent": normal_values(arg_keys[6], (NLAT, NLON, D), 1.0, 6.0, ((0, 4), (1, 8))),
    }


norm_eps = 1e-05
clip_eps = 1e-06
clip_level = 1.0
masked_score = -1e+30
highest = lax.Precision.HIGHEST

def widen(array_in):
    return array_in.astype(jnp.float32)

def relation_onehot(win_lat, win_lon):
    position = jnp.arange(win_lat * win_lon, dtype=jnp.int32)
    row_of = position // win_lon
    column = position % win_lon
    offset = (row_of[:, None] - row_of[None, :] + win_lat - 1) * (2 * win_lon - 1) + (column[:, None] - column[None, :] + win_lon - 1)
    extent = (2 * win_lat - 1) * (2 * win_lon - 1)
    return (offset.reshape(-1)[:, None] == jnp.arange(extent, dtype=jnp.int32)[None, :]).astype(jnp.float32)

def to_windows(source, win_lat, win_lon):
    rows_all, cols_all, channels = source.shape
    source = source.reshape(rows_all // win_lat, win_lat, cols_all // win_lon, win_lon, channels)
    return source.transpose(0, 2, 1, 3, 4).reshape(-1, win_lat * win_lon, channels)

def from_windows(windows, rows_all, cols_all, win_lat, win_lon):
    channels = windows.shape[-1]
    source = windows.reshape(rows_all // win_lat, cols_all // win_lon, win_lat, win_lon, channels)
    return source.transpose(0, 2, 1, 3, 4).reshape(rows_all, cols_all, channels)

def window_bias(bias_table, kinds_flat, onehot_rel, positions):
    kind_count, heads_n, extent = bias_table.shape
    spread = jnp.dot(bias_table.reshape(kind_count * heads_n, extent), onehot_rel.T, precision=highest, preferred_element_type=jnp.float32)
    kind_onehot = (kinds_flat[:, None] == jnp.arange(kind_count, dtype=jnp.int32)[None, :]).astype(jnp.float32)
    per_window = jnp.dot(kind_onehot, spread.reshape(kind_count, heads_n * positions * positions), precision=highest, preferred_element_type=jnp.float32)
    return (per_window.reshape(-1, heads_n, positions, positions), kind_onehot)

def attend_forward(x_windows, norm_gain, w_qkv, w_proj, bias_win, allowed):
    count, positions, channels = x_windows.shape
    head_size = channels // HEADS
    inv_sqrt = head_size ** (-0.5)
    flat_rows = x_windows.reshape(-1, channels).astype(jnp.float32)
    centre = flat_rows - lax.optimization_barrier(jnp.mean(flat_rows, axis=-1, keepdims=True))
    inverse = lax.rsqrt(lax.optimization_barrier(jnp.mean(centre * centre, axis=-1, keepdims=True)) + norm_eps)
    unit_rows = centre * inverse
    normed = (unit_rows * norm_gain).astype(jnp.bfloat16)
    qkv_rows = jnp.dot(normed, w_qkv, preferred_element_type=jnp.float32).astype(jnp.bfloat16)
    parts_qkv = qkv_rows.reshape(count, positions, 3, HEADS, head_size)
    queries = parts_qkv[:, :, 0]
    keys_in = parts_qkv[:, :, 1]
    values_in = parts_qkv[:, :, 2]
    scores = jnp.einsum('wihd,wjhd->whij', widen(queries), widen(keys_in), precision=highest) * inv_sqrt + bias_win
    scores = jnp.where(allowed, scores, masked_score)
    soft_probs = jax.nn.softmax(scores, axis=-1)
    probs_low = soft_probs.astype(jnp.bfloat16)
    mixed_rows = jnp.einsum('whij,wjhd->wihd', widen(probs_low), widen(values_in), precision=highest).astype(jnp.bfloat16).reshape(-1, channels)
    branch = jnp.dot(mixed_rows, w_proj, preferred_element_type=jnp.float32).astype(jnp.bfloat16)
    saved = (normed, unit_rows, inverse, queries, keys_in, values_in, soft_probs, probs_low, mixed_rows)
    return (saved, branch)

def attend_backward(saved, g_windows, keep_win, w_qkv, w_proj, norm_gain, kind_onehot, onehot_rel, table_dims):
    normed, unit_rows, inverse, queries, keys_in, values_in, soft_probs, probs_low, mixed_rows = saved
    count, heads_n, positions = (soft_probs.shape[0], soft_probs.shape[1], soft_probs.shape[2])
    channels = normed.shape[1]
    head_size = channels // heads_n
    inv_sqrt = head_size ** (-0.5)
    flat_g = g_windows.reshape(-1, channels)
    keep_rows = keep_win.reshape(-1, 1)
    keep_low = keep_rows.astype(jnp.bfloat16)
    grad_proj = jnp.dot((mixed_rows * keep_low).T, flat_g, preferred_element_type=jnp.float32)
    d_mixed = jnp.dot(flat_g, w_proj.T, preferred_element_type=jnp.float32).astype(jnp.bfloat16)
    d_mixed = d_mixed.reshape(count, positions, heads_n, head_size)
    d_probs = jnp.einsum('wihd,wjhd->whij', widen(d_mixed), widen(values_in), precision=highest)
    d_values = jnp.einsum('whij,wihd->wjhd', widen(probs_low), widen(d_mixed), precision=highest).astype(jnp.bfloat16)
    d_scores = soft_probs * (d_probs - lax.optimization_barrier(jnp.sum(soft_probs * d_probs, axis=-1, keepdims=True)))
    d_scores_low = d_scores.astype(jnp.bfloat16)
    d_queries = (jnp.einsum('whij,wjhd->wihd', widen(d_scores_low), widen(keys_in), precision=highest) * inv_sqrt).astype(jnp.bfloat16)
    d_keys = (jnp.einsum('whij,wihd->wjhd', widen(d_scores_low), widen(queries), precision=highest) * inv_sqrt).astype(jnp.bfloat16)
    d_qkv = jnp.stack([d_queries, d_keys, d_values], axis=2).reshape(-1, 3 * channels)
    grad_qkv = jnp.dot((normed * keep_low).T, d_qkv, preferred_element_type=jnp.float32)
    d_normed = jnp.dot(d_qkv, w_qkv.T, preferred_element_type=jnp.float32)
    grad_gain = lax.optimization_barrier(jnp.sum(d_normed * unit_rows * keep_rows, axis=0))
    d_unit = d_normed * norm_gain
    d_path = inverse * (d_unit - lax.optimization_barrier(jnp.mean(d_unit, axis=-1, keepdims=True)) - unit_rows * lax.optimization_barrier(jnp.mean(d_unit * unit_rows, axis=-1, keepdims=True)))
    d_path = d_path.astype(jnp.bfloat16)
    query_keep = keep_win.reshape(count, 1, positions, 1)
    by_kind = jnp.dot(kind_onehot.T, (d_scores * query_keep).reshape(count, -1), precision=highest, preferred_element_type=jnp.float32)
    grad_table = jnp.dot(by_kind.reshape(-1, positions * positions), onehot_rel, precision=highest, preferred_element_type=jnp.float32)
    return (d_path, (grad_qkv, grad_proj, grad_table.reshape(table_dims), grad_gain))

def clip_rms(gradient):
    return gradient * jnp.minimum(1.0, clip_level * lax.rsqrt(jnp.mean(gradient * gradient) + clip_eps))

def reference(state_grid, norm_gain, w_qkv, w_proj, bias_table, window_kind, cotangent):
    rows_all, cols_all, channels = state_grid.shape
    half_lat = WIN_LAT // 2
    half_lon = WIN_LON // 2
    positions = WIN_LAT * WIN_LON
    onehot_rel = relation_onehot(WIN_LAT, WIN_LON)
    rolled_x = jnp.roll(state_grid, (-half_lat, -half_lon), axis=(0, 1))
    rolled_g = jnp.roll(cotangent, (-half_lat, -half_lon), axis=(0, 1))
    stacked_x = rolled_x.reshape(BANDS, WIN_LAT, cols_all, channels)
    stacked_g = rolled_g.reshape(BANDS, WIN_LAT, cols_all, channels)
    row_index = jnp.arange(rows_all, dtype=jnp.int32)
    labels_all = (((row_index + half_lat) % rows_all + half_lat) // WIN_LAT).reshape(BANDS, WIN_LAT)

    def band_step(running, slab_in):
        band_x, band_g, band_kinds, band_labels = slab_in
        label_grid = jnp.broadcast_to(band_labels[:, None, None], (WIN_LAT, cols_all, 1))
        label_win = to_windows(label_grid, WIN_LAT, WIN_LON)[:, :, 0]
        allowed = (label_win[:, :, None] == label_win[:, None, :])[:, None]
        bias_win, kind_onehot = window_bias(bias_table, band_kinds, onehot_rel, positions)
        saved, branch = attend_forward(to_windows(band_x, WIN_LAT, WIN_LON), norm_gain, w_qkv, w_proj, bias_win, allowed)
        keep_win = jnp.ones(label_win.shape, jnp.float32)
        g_windows = to_windows(band_g, WIN_LAT, WIN_LON)
        d_path, grads = attend_backward(saved, g_windows, keep_win, w_qkv, w_proj, norm_gain, kind_onehot, onehot_rel, bias_table.shape)
        running = tuple((earlier + gradient for earlier, gradient in zip(running, grads)))
        branch_band = from_windows(branch.reshape(-1, positions, channels), WIN_LAT, cols_all, WIN_LAT, WIN_LON)
        path_band = from_windows(d_path.reshape(-1, positions, channels), WIN_LAT, cols_all, WIN_LAT, WIN_LON)
        return (running, (branch_band, path_band))
    zeros_init = (jnp.zeros((channels, 3 * channels), jnp.float32), jnp.zeros((channels, channels), jnp.float32), jnp.zeros(bias_table.shape, jnp.float32), jnp.zeros((channels,), jnp.float32))
    running, (branch_all, path_all) = lax.scan(band_step, zeros_init, (stacked_x, stacked_g, window_kind, labels_all))
    branch_all = jnp.roll(branch_all.reshape(rows_all, cols_all, channels), (half_lat, half_lon), axis=(0, 1))
    path_all = jnp.roll(path_all.reshape(rows_all, cols_all, channels), (half_lat, half_lon), axis=(0, 1))
    out_field = (state_grid.astype(jnp.float32) + branch_all.astype(jnp.float32)).astype(jnp.bfloat16)
    d_field = (cotangent.astype(jnp.float32) + path_all.astype(jnp.float32)).astype(jnp.bfloat16)
    return (out_field, d_field, clip_rms(running[0]), clip_rms(running[1]), clip_rms(running[2]), clip_rms(running[3]))
```

```python
import functools

import jax
import jax.numpy as jnp
from jax import lax
from jax.experimental import pallas as pl
from jax.experimental.pallas import tpu as pltpu
from jax.sharding import PartitionSpec as P

HEADS = 6
WIN_LAT = 6
WIN_LON = 12
HALF_LAT = 3
HALF_LON = 6
PAD = 8
SPAN = 2 * WIN_LON - 1
TOP = (WIN_LAT - 1) * SPAN + WIN_LON - 1

norm_eps = 1e-05
clip_eps = 1e-06
masked_score = -1e30
f32 = jnp.float32
bf16 = jnp.bfloat16
MESH = pl.DeviceIdType.MESH
VM = pl.BlockSpec(memory_space=pltpu.VMEM)


def nt(a, b):
    return lax.dot_general(a, b, (((1,), (1,)), ((), ())), preferred_element_type=f32)


def tn(a, b):
    return lax.dot_general(a, b, (((0,), (0,)), ((), ())), preferred_element_type=f32)


def nn(a, b):
    return jnp.dot(a, b, preferred_element_type=f32)


def halo_kernel(nlat, nlon, own_ref, out_ref, sends, recvs, local):
    lat = lax.axis_index("lat")
    lon = lax.axis_index("lon")
    last = own_ref.shape[1] - 1
    up, down = lax.rem(lat + nlat - 1, nlat), lax.rem(lat + 1, nlat)
    left, right = lax.rem(lon + nlon - 1, nlon), lax.rem(lon + 1, nlon)
    barrier = pltpu.get_barrier_semaphore()
    for who in ((down, lon), (lat, right), (down, right)):
        pl.semaphore_signal(barrier, inc=1, device_id=who, device_id_type=MESH)
    pl.semaphore_wait(barrier, 3)
    top = pl.ds(0, HALF_LAT)
    bottom = pl.ds(HALF_LAT, HALF_LAT)
    inner = pl.ds(1, last)
    moves = (
        (own_ref.at[top, inner], out_ref.at[top, pl.ds(0, last)], (up, lon)),
        (own_ref.at[top, pl.ds(0, 1)], out_ref.at[top, pl.ds(last, 1)], (up, left)),
        (own_ref.at[bottom, pl.ds(0, 1)], out_ref.at[bottom, pl.ds(last, 1)], (lat, left)),
    )
    copies = [
        pltpu.make_async_remote_copy(
            src_ref=src, dst_ref=dst, send_sem=sends.at[i], recv_sem=recvs.at[i],
            device_id=who, device_id_type=MESH,
        )
        for i, (src, dst, who) in enumerate(moves)
    ]
    for copy in copies:
        copy.start()
    keep = pltpu.make_async_copy(
        own_ref.at[bottom, inner], out_ref.at[bottom, pl.ds(0, last)], local
    )
    keep.start()
    keep.wait()
    for copy in copies:
        copy.wait()


def attend_kernel(
    kinds_ref, joint_ref, gain_ref, wqkv_ref, wproj_ref, bias_ref,
    res_ref, pieces_ref,
    unit_ref, inv_ref, normed_ref, qkv_ref, dmix_ref, g_ref, mixed_ref, dqkv_ref,
    neg_ref, emb_ref, table_in, table_ref, grad_ref,
):
    lat = lax.axis_index("lat")
    lon = lax.axis_index("lon")
    nlat = lax.axis_size("lat")
    _, windows, wide, twice = joint_ref.shape
    channels = twice // 2
    tokens = WIN_LAT * wide
    head = channels // HEADS
    inv_sqrt = head ** (-0.5)
    total = WIN_LAT * windows * wide
    four = (WIN_LAT, windows, wide)

    x = joint_ref[:, :, :, :channels].reshape(total, channels).astype(f32)
    g = joint_ref[:, :, :, channels:].reshape(total, channels)
    g_ref[...] = g
    centre = x - jnp.mean(x, axis=-1, keepdims=True)
    inverse = lax.rsqrt(jnp.mean(centre * centre, axis=-1, keepdims=True) + norm_eps)
    unit = centre * inverse
    unit_ref[...] = unit
    inv_ref[...] = inverse
    normed = (unit * gain_ref[...]).astype(bf16)
    normed_ref[...] = normed
    qkv_ref[...] = nn(normed, wqkv_ref[...]).astype(bf16).reshape(four + (3 * channels,))
    dmix_ref[...] = nt(g, wproj_ref[...]).astype(bf16).reshape(four + (channels,))

    def place(index):
        slot = index >> 4
        row = jnp.where(slot >= HALF_LAT, slot - HALF_LAT, slot + HALF_LAT)
        side = (index >> 3) & 1
        column = index & 7
        return row, column, SPAN * row + HALF_LON * side + column

    row_i, _, _ = place(lax.broadcasted_iota(jnp.int32, (tokens, 128), 0))
    lane = TOP - lax.broadcasted_iota(jnp.int32, (tokens, 128), 1)
    good = lane > TOP
    for row in range(WIN_LAT):
        start = SPAN * row
        fits = (lane >= start) & (lane < start + WIN_LON)
        same = (row_i < HALF_LAT) if row < HALF_LAT else (row_i >= HALF_LAT)
        good = good | (fits & (same | (lat < nlat - 1)))
    neg_ref[...] = jnp.where(good, 0.0, masked_score)
    slot_j, column_j, place_j = place(lax.broadcasted_iota(jnp.int32, (128, tokens), 1))
    spot = TOP - lax.broadcasted_iota(jnp.int32, (128, tokens), 0)
    emb_ref[...] = jnp.where((spot == place_j) & (column_j < HALF_LON), 1.0, 0.0).astype(bf16)

    table_in[...] = jnp.zeros_like(table_in)
    table_in[:, :, : bias_ref.shape[2]] = bias_ref[...]
    table_ref[...] = jnp.zeros_like(table_ref)

    lane8 = lax.broadcasted_iota(jnp.int32, (PAD, 128), 1)
    sub8 = lax.broadcasted_iota(jnp.int32, (PAD, 256), 0)
    head_of = lax.broadcasted_iota(jnp.int32, (1, channels), 1) // head
    masks = [(head_of == h).astype(bf16) for h in range(HEADS)]
    masks32 = [(head_of == h).astype(f32) for h in range(HEADS)]
    bases = []
    for block in range(tokens // PAD):
        slot, side = block // 2, block % 2
        bases.append(SPAN * ((slot + HALF_LAT) % WIN_LAT) + HALF_LON * side)

    @pl.loop(0, windows)
    def _(w):
        kind = kinds_ref[lat, lon * windows + w]
        qkv = qkv_ref[:, w].reshape(tokens, 3 * channels)
        queries = qkv[:, :channels]
        emb = emb_ref[...]
        kv = nn(emb, qkv[:, channels:]).astype(bf16)
        keys, values = kv[:, :channels], kv[:, channels:]
        dmix = dmix_ref[:, w].reshape(tokens, channels)
        q_all = jnp.concatenate([queries * m for m in masks], axis=0)
        d_all = jnp.concatenate([dmix * m for m in masks], axis=0)
        raw = nt(q_all, keys)
        rows = table_in[kind]
        parts = []
        for h in range(HEADS):
            base = jnp.broadcast_to(rows[h : h + 1], (PAD, 256))
            for bit in (1, 2, 4):
                base = jnp.where((sub8 & bit) != 0, pltpu.roll(base, 256 - bit, 1), base)
            low, high = base[:, :128], base[:, 128:]
            for shift in bases:
                if shift == 0:
                    parts.append(low)
                else:
                    parts.append(
                        jnp.where(
                            lane8 < 128 - shift,
                            pltpu.roll(low, 128 - shift, 1),
                            pltpu.roll(high, 128 - shift, 1),
                        )
                    )
        bias = jnp.concatenate(parts, axis=0)
        neg = neg_ref[...]
        scores = raw * inv_sqrt + bias + jnp.concatenate([neg] * HEADS, axis=0)
        expo = jnp.exp(scores - jnp.max(scores, axis=-1, keepdims=True))
        probs = expo * (1.0 / jnp.sum(expo, axis=-1, keepdims=True))
        low_p = probs.astype(bf16)

        def fold(stacked):
            out = stacked[:tokens] * masks32[0]
            for h in range(1, HEADS):
                out = out + stacked[h * tokens : (h + 1) * tokens] * masks32[h]
            return out

        mixed_ref[:, w] = fold(nn(low_p, values)).astype(bf16).reshape(WIN_LAT, wide, channels)
        d_probs = nt(d_all, values)
        d_scores = probs * (d_probs - jnp.sum(probs * d_probs, axis=-1, keepdims=True))
        low_d = d_scores.astype(bf16)
        d_q = (fold(nn(low_d, keys)) * inv_sqrt).astype(bf16)
        d_k = (tn(low_d, q_all) * inv_sqrt).astype(bf16)
        d_v = tn(low_p, d_all).astype(bf16)
        d_kv = tn(emb, jnp.concatenate([d_k, d_v], axis=1)).astype(bf16)
        dqkv_ref[:, w] = jnp.concatenate([d_q, d_kv], axis=1).reshape(WIN_LAT, wide, 3 * channels)
        for h in range(HEADS):
            low = jnp.zeros((PAD, 128), f32)
            high = jnp.zeros((PAD, 128), f32)
            for block, shift in enumerate(bases):
                at = h * tokens + block * PAD
                tile = d_scores[at : at + PAD]
                if shift == 0:
                    low = low + tile
                else:
                    turned = pltpu.roll(tile, shift, 1)
                    low = low + jnp.where(lane8 >= shift, turned, 0.0)
                    high = high + jnp.where(lane8 < shift, turned, 0.0)
            table_ref[kind, h] += jnp.concatenate([low, high], axis=1)

    mixed = mixed_ref[...].reshape(total, channels)
    d_qkv = dqkv_ref[...].reshape(total, 3 * channels)
    branch = nn(mixed, wproj_ref[...])
    d_normed = nt(d_qkv, wqkv_ref[...])
    unit = unit_ref[...]
    grad_ref[:, : 3 * channels] = tn(normed_ref[...], d_qkv)
    grad_ref[:, 3 * channels :] = tn(mixed, g_ref[...])
    gain_grad = jnp.sum(d_normed * unit, axis=0, keepdims=True)
    d_unit = d_normed * gain_ref[...]
    path = inv_ref[...] * (
        d_unit
        - jnp.mean(d_unit, axis=-1, keepdims=True)
        - unit * jnp.mean(d_unit * unit, axis=-1, keepdims=True)
    )
    res_ref[:, :, :, :channels] = branch.astype(bf16).reshape(four + (channels,))
    res_ref[:, :, :, channels:] = path.astype(bf16).reshape(four + (channels,))

    table = table_ref[...]
    sub = lax.broadcasted_iota(jnp.int32, table.shape, 2)
    flat = table.reshape(-1, 256)
    sub = sub.reshape(-1, 256)
    for bit in (1, 2, 4):
        flat = jnp.where((sub & bit) != 0, pltpu.roll(flat, bit, 1), flat)
    binned = jnp.sum(flat.reshape(table.shape[0] * HEADS, PAD, 256), axis=1)

    pieces_ref[...] = jnp.zeros_like(pieces_ref)
    count = 0
    for column in range(4 * channels // 128):
        part = grad_ref[:, column * 128 : (column + 1) * 128].astype(bf16)
        pieces_ref[count : count + channels // 16] = part.reshape(channels // 16, 16, 128)
        count += channels // 16
    rows_t = binned.shape[0] // 16
    for side in range(2):
        part = binned[:, side * 128 : (side + 1) * 128].astype(bf16)
        pieces_ref[count : count + rows_t] = part.reshape(rows_t, 16, 128)
        count += rows_t
    gain_low = gain_grad.astype(bf16)
    pieces_ref[count, 0:1, :] = gain_low[:, :128]
    pieces_ref[count, 1:2, : channels - 128] = gain_low[:, 128:]


def finish_kernel(
    nlat, nlon, res_ref, own_ref, pieces_ref,
    both_ref, qkv_ref, proj_ref, table_ref, gain_ref,
    land_ref, rs_ref, red_ref, ag_ref, grad_ref,
    sends, recvs, rs_send, rs_recv, ag_send, ag_recv,
):
    lat = lax.axis_index("lat")
    lon = lax.axis_index("lon")
    count = nlat * nlon
    me = lat * nlon + lon
    share = red_ref.shape[0]
    last = own_ref.shape[1] - 1
    down, right = lax.rem(lat + 1, nlat), lax.rem(lon + 1, nlon)

    def peer(step):
        who = lax.rem(me + step, count)
        return who, (lax.div(who, nlon), lax.rem(who, nlon))

    barrier = pltpu.get_barrier_semaphore()

    @pl.loop(1, count)
    def _(step):
        pl.semaphore_signal(barrier, inc=1, device_id=peer(step)[1], device_id_type=MESH)

    pl.semaphore_wait(barrier, count - 1)

    def scatter(step):
        who, where = peer(step)
        return pltpu.make_async_remote_copy(
            src_ref=pieces_ref.at[pl.ds(who * share, share)],
            dst_ref=rs_ref.at[pl.ds((step - 1) * share, share)],
            send_sem=rs_send, recv_sem=rs_recv, device_id=where, device_id_type=MESH,
        )

    @pl.loop(1, count)
    def _(step):
        scatter(step).start()

    top = pl.ds(0, HALF_LAT)
    bottom = pl.ds(HALF_LAT, HALF_LAT)
    moves = (
        (res_ref.at[top, pl.ds(0, last)], land_ref.at[top, pl.ds(1, last)], (down, lon)),
        (res_ref.at[top, pl.ds(last, 1)], land_ref.at[top, pl.ds(0, 1)], (down, right)),
        (res_ref.at[bottom, pl.ds(last, 1)], land_ref.at[bottom, pl.ds(0, 1)], (lat, right)),
    )
    copies = [
        pltpu.make_async_remote_copy(
            src_ref=src, dst_ref=dst, send_sem=sends.at[i], recv_sem=recvs.at[i],
            device_id=who, device_id_type=MESH,
        )
        for i, (src, dst, who) in enumerate(moves)
    ]
    for copy in copies:
        copy.start()

    pltpu.make_async_copy(rs_ref, rs_ref, rs_recv).wait()
    summed = pieces_ref[pl.ds(me * share, share)].astype(f32)

    def add(step, running):
        return running + rs_ref[pl.ds(step * share, share)].astype(f32)

    summed = lax.fori_loop(0, count - 1, add, summed)
    red_ref[...] = summed.astype(bf16)

    def gather(step):
        return pltpu.make_async_remote_copy(
            src_ref=red_ref, dst_ref=ag_ref.at[pl.ds(me * share, share)],
            send_sem=ag_send, recv_sem=ag_recv, device_id=peer(step)[1], device_id_type=MESH,
        )

    @pl.loop(1, count)
    def _(step):
        gather(step).start()

    ag_ref[pl.ds(me * share, share)] = summed.astype(bf16)

    own_part = own_ref[bottom, 1:].astype(f32) + res_ref[bottom, :last].astype(f32)
    both_ref[bottom, 1:] = own_part.astype(bf16)
    for copy in copies:
        copy.wait()
    both_ref[top] = (own_ref[top].astype(f32) + land_ref[top].astype(f32)).astype(bf16)
    both_ref[bottom, 0:1] = (
        own_ref[bottom, 0:1].astype(f32) + land_ref[bottom, 0:1].astype(f32)
    ).astype(bf16)

    pltpu.make_async_copy(rs_ref, rs_ref, ag_recv).wait()
    channels = gain_ref.shape[1]
    at = 0
    for column in range(4 * channels // 128):
        part = ag_ref[at : at + channels // 16].astype(f32)
        grad_ref[:, column * 128 : (column + 1) * 128] = part.reshape(channels, 128)
        at += channels // 16
    kinds, heads, extent = table_ref.shape
    rows_t = kinds * heads // 16
    sides = []
    for side in range(2):
        sides.append(ag_ref[at : at + rows_t].astype(f32).reshape(kinds * heads, 128))
        at += rows_t
    table = jnp.concatenate(sides, axis=1)
    gain_block = ag_ref[at].astype(f32)
    gain = jnp.concatenate([gain_block[0:1], gain_block[1:2, : channels - 128]], axis=1)

    def scale(value, entries):
        mean = jnp.sum(jnp.sum(value * value, axis=1, keepdims=True), axis=0, keepdims=True)
        return jnp.minimum(1.0, lax.rsqrt(mean * (1.0 / entries) + clip_eps))

    wide = grad_ref[:, : 3 * channels]
    qkv_ref[...] = wide * scale(wide, wide.size)
    proj = grad_ref[:, 3 * channels :]
    proj_ref[...] = proj * scale(proj, proj.size)
    lane = lax.broadcasted_iota(jnp.int32, table.shape, 1)
    table = jnp.where(lane < extent, table, 0.0)
    table = table * scale(table, kinds * heads * extent)
    for kind in range(kinds):
        table_ref[kind] = table[kind * heads : (kind + 1) * heads, :extent]
    gain_ref[...] = gain * scale(gain, channels)

    pltpu.make_async_copy(rs_ref, rs_ref, rs_send).wait()
    pltpu.make_async_copy(rs_ref, rs_ref, ag_send).wait()


def on_device(nlat, nlon, state_grid, norm_gain, w_qkv, w_proj, bias_table, window_kind, cotangent):
    rows_dev, cols_dev, channels = state_grid.shape
    halves = cols_dev // HALF_LON
    windows = cols_dev // WIN_LON
    kinds, heads, extent = bias_table.shape
    devices = nlat * nlon
    joint = jnp.concatenate([state_grid, cotangent], axis=2)
    joint = joint.reshape(rows_dev, halves, HALF_LON, 2 * channels)
    joint = jnp.pad(joint, ((0, 0), (0, 0), (0, PAD - HALF_LON), (0, 0)))
    grid_shape = joint.shape

    block = pl.pallas_call(
        functools.partial(halo_kernel, nlat, nlon),
        name="halo",
        out_shape=jax.ShapeDtypeStruct(grid_shape, bf16),
        in_specs=[VM],
        out_specs=VM,
        scratch_shapes=[
            pltpu.SemaphoreType.DMA((3,)),
            pltpu.SemaphoreType.DMA((3,)),
            pltpu.SemaphoreType.DMA(()),
        ],
        compiler_params=pltpu.CompilerParams(collective_id=0, has_side_effects=True),
    )(joint)

    wide = 2 * PAD
    four = (WIN_LAT, windows, wide)
    total = WIN_LAT * windows * wide
    tokens = WIN_LAT * wide
    used = 4 * channels // 128 * (channels // 16) + 2 * (kinds * heads // 16) + 1
    share = -(-used // devices)
    res, pieces = pl.pallas_call(
        attend_kernel,
        name="attend",
        out_shape=(
            jax.ShapeDtypeStruct(four + (2 * channels,), bf16),
            jax.ShapeDtypeStruct((share * devices, 16, 128), bf16),
        ),
        in_specs=[pl.BlockSpec(memory_space=pltpu.SMEM)] + [VM] * 5,
        out_specs=(VM, VM),
        scratch_shapes=[
            pltpu.VMEM((total, channels), f32),
            pltpu.VMEM((total, 1), f32),
            pltpu.VMEM((total, channels), bf16),
            pltpu.VMEM(four + (3 * channels,), bf16),
            pltpu.VMEM(four + (channels,), bf16),
            pltpu.VMEM((total, channels), bf16),
            pltpu.VMEM(four + (channels,), bf16),
            pltpu.VMEM(four + (3 * channels,), bf16),
            pltpu.VMEM((tokens, 128), f32),
            pltpu.VMEM((128, tokens), bf16),
            pltpu.VMEM((kinds, heads, 256), f32),
            pltpu.VMEM((kinds, heads, PAD, 256), f32),
            pltpu.VMEM((channels, 4 * channels), f32),
        ],
    )(
        window_kind,
        block.reshape(four + (2 * channels,)),
        norm_gain.reshape(1, channels),
        w_qkv,
        w_proj,
        bias_table,
    )

    both, qkv_grad, proj_grad, table_grad, gain_grad = pl.pallas_call(
        functools.partial(finish_kernel, nlat, nlon),
        name="finish",
        out_shape=(
            jax.ShapeDtypeStruct(grid_shape, bf16),
            jax.ShapeDtypeStruct((channels, 3 * channels), f32),
            jax.ShapeDtypeStruct((channels, channels), f32),
            jax.ShapeDtypeStruct((kinds, heads, extent), f32),
            jax.ShapeDtypeStruct((1, channels), f32),
        ),
        in_specs=[VM] * 3,
        out_specs=(VM,) * 5,
        scratch_shapes=[
            pltpu.VMEM(grid_shape, bf16),
            pltpu.VMEM((share * (devices - 1), 16, 128), bf16),
            pltpu.VMEM((share, 16, 128), bf16),
            pltpu.VMEM((share * devices, 16, 128), bf16),
            pltpu.VMEM((channels, 4 * channels), f32),
            pltpu.SemaphoreType.DMA((3,)),
            pltpu.SemaphoreType.DMA((3,)),
            pltpu.SemaphoreType.DMA(()),
            pltpu.SemaphoreType.DMA(()),
            pltpu.SemaphoreType.DMA(()),
            pltpu.SemaphoreType.DMA(()),
        ],
        compiler_params=pltpu.CompilerParams(collective_id=1, has_side_effects=True),
    )(res.reshape(grid_shape), joint, pieces)

    both = both[:, :, :HALF_LON].reshape(rows_dev, cols_dev, 2 * channels)
    return (
        both[:, :, :channels],
        both[:, :, channels:],
        qkv_grad,
        proj_grad,
        table_grad,
        gain_grad.reshape(channels),
    )


def solution(mesh):
    in_specs = (P("lat", "lon", None), P(), P(), P(), P(), P(), P("lat", "lon", None))
    out_specs = (P("lat", "lon", None), P("lat", "lon", None), P(), P(), P(), P())
    body = functools.partial(on_device, mesh.shape["lat"], mesh.shape["lon"])
    return jax.shard_map(body, mesh=mesh, in_specs=in_specs, out_specs=out_specs, check_vma=False)
```

```python
import functools

import jax
import jax.numpy as jnp
from jax import lax
from jax.experimental import pallas as pl
from jax.experimental.pallas import tpu as pltpu
from jax.sharding import PartitionSpec as P

HEADS = 6
WIN_LAT = 6
WIN_LON = 12
HALF_LAT = 3
HALF_LON = 6
PAD = 8
ROWS = 8
SPAN = 2 * WIN_LON - 1
TOP = (WIN_LAT - 1) * SPAN + WIN_LON - 1

norm_eps = 1e-05
clip_eps = 1e-06
masked_score = -1e30
f32 = jnp.float32
bf16 = jnp.bfloat16
MESH = pl.DeviceIdType.MESH
VM = pl.BlockSpec(memory_space=pltpu.VMEM)


def nt(a, b):
    return lax.dot_general(a, b, (((1,), (1,)), ((), ())), preferred_element_type=f32)


def tn(a, b):
    return lax.dot_general(a, b, (((0,), (0,)), ((), ())), preferred_element_type=f32)


def nn(a, b):
    return jnp.dot(a, b, preferred_element_type=f32)


def halo_kernel(nlat, nlon, own_ref, out_ref, sends, recvs, local):
    lat = lax.axis_index("lat")
    lon = lax.axis_index("lon")
    last = own_ref.shape[1] - 1
    up, down = lax.rem(lat + nlat - 1, nlat), lax.rem(lat + 1, nlat)
    left, right = lax.rem(lon + nlon - 1, nlon), lax.rem(lon + 1, nlon)
    barrier = pltpu.get_barrier_semaphore()
    for who in ((down, lon), (lat, right), (down, right)):
        pl.semaphore_signal(barrier, inc=1, device_id=who, device_id_type=MESH)
    pl.semaphore_wait(barrier, 3)
    top = pl.ds(0, HALF_LAT)
    bottom = pl.ds(HALF_LAT, HALF_LAT)
    inner = pl.ds(1, last)
    moves = (
        (own_ref.at[top, inner], out_ref.at[top, pl.ds(0, last)], (up, lon)),
        (own_ref.at[top, pl.ds(0, 1)], out_ref.at[top, pl.ds(last, 1)], (up, left)),
        (own_ref.at[bottom, pl.ds(0, 1)], out_ref.at[bottom, pl.ds(last, 1)], (lat, left)),
    )
    copies = [
        pltpu.make_async_remote_copy(
            src_ref=src, dst_ref=dst, send_sem=sends.at[i], recv_sem=recvs.at[i],
            device_id=who, device_id_type=MESH,
        )
        for i, (src, dst, who) in enumerate(moves)
    ]
    for copy in copies:
        copy.start()
    keep = pltpu.make_async_copy(
        own_ref.at[bottom, inner], out_ref.at[bottom, pl.ds(0, last)], local
    )
    keep.start()
    keep.wait()
    for copy in copies:
        copy.wait()


def attend_kernel(
    kinds_ref, joint_ref, gain_ref, wqkv_ref, wproj_ref, bias_ref,
    res_ref, pieces_ref,
    unit_ref, inv_ref, normed_ref, qkv_ref, dmix_ref, g_ref, mixed_ref, dqkv_ref,
    neg_ref, emb_ref, table_in, table_ref, grad_ref,
):
    lat = lax.axis_index("lat")
    lon = lax.axis_index("lon")
    nlat = lax.axis_size("lat")
    _, windows, wide, twice = joint_ref.shape
    channels = twice // 2
    tokens = WIN_LAT * wide
    head = channels // HEADS
    inv_sqrt = head ** (-0.5)
    total = WIN_LAT * windows * wide
    four = (WIN_LAT, windows, wide)

    x = joint_ref[:, :, :, :channels].reshape(total, channels).astype(f32)
    g = joint_ref[:, :, :, channels:].reshape(total, channels)
    g_ref[...] = g
    centre = x - jnp.mean(x, axis=-1, keepdims=True)
    inverse = lax.rsqrt(jnp.mean(centre * centre, axis=-1, keepdims=True) + norm_eps)
    unit = centre * inverse
    unit_ref[...] = unit
    inv_ref[...] = inverse
    normed = (unit * gain_ref[...]).astype(bf16)
    normed_ref[...] = normed
    qkv_ref[...] = nn(normed, wqkv_ref[...]).astype(bf16).reshape(four + (3 * channels,))
    dmix_ref[...] = nt(g, wproj_ref[...]).astype(bf16).reshape(four + (channels,))

    def place(index):
        slot = index >> 4
        row = jnp.where(slot >= HALF_LAT, slot - HALF_LAT, slot + HALF_LAT)
        side = (index >> 3) & 1
        column = index & 7
        return row, column, SPAN * row + HALF_LON * side + column

    row_i, _, _ = place(lax.broadcasted_iota(jnp.int32, (tokens, 128), 0))
    lane = TOP - lax.broadcasted_iota(jnp.int32, (tokens, 128), 1)
    good = lane > TOP
    for row in range(WIN_LAT):
        start = SPAN * row
        fits = (lane >= start) & (lane < start + WIN_LON)
        same = (row_i < HALF_LAT) if row < HALF_LAT else (row_i >= HALF_LAT)
        good = good | (fits & (same | (lat < nlat - 1)))
    neg_ref[...] = jnp.where(good, 0.0, masked_score)
    slot_j, column_j, place_j = place(lax.broadcasted_iota(jnp.int32, (128, tokens), 1))
    spot = TOP - lax.broadcasted_iota(jnp.int32, (128, tokens), 0)
    emb_ref[...] = jnp.where((spot == place_j) & (column_j < HALF_LON), 1.0, 0.0).astype(bf16)

    table_in[...] = jnp.zeros_like(table_in)
    table_in[:, :, : bias_ref.shape[2]] = bias_ref[...]
    table_ref[...] = jnp.zeros_like(table_ref)

    lane8 = lax.broadcasted_iota(jnp.int32, (PAD, 128), 1)
    sub8 = lax.broadcasted_iota(jnp.int32, (PAD, 256), 0)
    head_of = lax.broadcasted_iota(jnp.int32, (1, channels), 1) // head
    masks = [(head_of == h).astype(bf16) for h in range(HEADS)]
    masks32 = [(head_of == h).astype(f32) for h in range(HEADS)]
    bases = []
    for block in range(tokens // PAD):
        slot, side = block // 2, block % 2
        bases.append(SPAN * ((slot + HALF_LAT) % WIN_LAT) + HALF_LON * side)

    @pl.loop(0, windows)
    def _(w):
        kind = kinds_ref[lat, lon * windows + w]
        qkv = qkv_ref[:, w].reshape(tokens, 3 * channels)
        queries = qkv[:, :channels]
        emb = emb_ref[...]
        kv = nn(emb, qkv[:, channels:]).astype(bf16)
        keys, values = kv[:, :channels], kv[:, channels:]
        dmix = dmix_ref[:, w].reshape(tokens, channels)
        q_all = jnp.concatenate([queries * m for m in masks], axis=0)
        d_all = jnp.concatenate([dmix * m for m in masks], axis=0)
        raw = nt(q_all, keys)
        rows = table_in[kind]
        parts = []
        for h in range(HEADS):
            base = jnp.broadcast_to(rows[h : h + 1], (PAD, 256))
            for bit in (1, 2, 4):
                base = jnp.where((sub8 & bit) != 0, pltpu.roll(base, 256 - bit, 1), base)
            low, high = base[:, :128], base[:, 128:]
            for shift in bases:
                if shift == 0:
                    parts.append(low)
                else:
                    parts.append(
                        jnp.where(
                            lane8 < 128 - shift,
                            pltpu.roll(low, 128 - shift, 1),
                            pltpu.roll(high, 128 - shift, 1),
                        )
                    )
        bias = jnp.concatenate(parts, axis=0)
        neg = neg_ref[...]
        scores = raw * inv_sqrt + bias + jnp.concatenate([neg] * HEADS, axis=0)
        expo = jnp.exp(scores - jnp.max(scores, axis=-1, keepdims=True))
        probs = expo * (1.0 / jnp.sum(expo, axis=-1, keepdims=True))
        low_p = probs.astype(bf16)

        def fold(stacked):
            out = stacked[:tokens] * masks32[0]
            for h in range(1, HEADS):
                out = out + stacked[h * tokens : (h + 1) * tokens] * masks32[h]
            return out

        mixed_ref[:, w] = fold(nn(low_p, values)).astype(bf16).reshape(WIN_LAT, wide, channels)
        d_probs = nt(d_all, values)
        d_scores = probs * (d_probs - jnp.sum(probs * d_probs, axis=-1, keepdims=True))
        low_d = d_scores.astype(bf16)
        d_q = (fold(nn(low_d, keys)) * inv_sqrt).astype(bf16)
        d_k = (tn(low_d, q_all) * inv_sqrt).astype(bf16)
        d_v = tn(low_p, d_all).astype(bf16)
        d_kv = tn(emb, jnp.concatenate([d_k, d_v], axis=1)).astype(bf16)
        dqkv_ref[:, w] = jnp.concatenate([d_q, d_kv], axis=1).reshape(WIN_LAT, wide, 3 * channels)
        for h in range(HEADS):
            low = jnp.zeros((PAD, 128), f32)
            high = jnp.zeros((PAD, 128), f32)
            for block, shift in enumerate(bases):
                at = h * tokens + block * PAD
                tile = d_scores[at : at + PAD]
                if shift == 0:
                    low = low + tile
                else:
                    turned = pltpu.roll(tile, shift, 1)
                    low = low + jnp.where(lane8 >= shift, turned, 0.0)
                    high = high + jnp.where(lane8 < shift, turned, 0.0)
            table_ref[kind, h] += jnp.concatenate([low, high], axis=1)

    mixed = mixed_ref[...].reshape(total, channels)
    d_qkv = dqkv_ref[...].reshape(total, 3 * channels)
    branch = nn(mixed, wproj_ref[...])
    d_normed = nt(d_qkv, wqkv_ref[...])
    unit = unit_ref[...]
    grad_ref[:, : 3 * channels] = tn(normed_ref[...], d_qkv)
    grad_ref[:, 3 * channels :] = tn(mixed, g_ref[...])
    gain_grad = jnp.sum(d_normed * unit, axis=0, keepdims=True)
    d_unit = d_normed * gain_ref[...]
    path = inv_ref[...] * (
        d_unit
        - jnp.mean(d_unit, axis=-1, keepdims=True)
        - unit * jnp.mean(d_unit * unit, axis=-1, keepdims=True)
    )
    res_ref[:, :, :, :channels] = branch.astype(bf16).reshape(four + (channels,))
    res_ref[:, :, :, channels:] = path.astype(bf16).reshape(four + (channels,))

    table = table_ref[...]
    sub = lax.broadcasted_iota(jnp.int32, table.shape, 2)
    flat = table.reshape(-1, 256)
    sub = sub.reshape(-1, 256)
    for bit in (1, 2, 4):
        flat = jnp.where((sub & bit) != 0, pltpu.roll(flat, bit, 1), flat)
    binned = jnp.sum(flat.reshape(table.shape[0] * HEADS, PAD, 256), axis=1)

    pieces_ref[...] = jnp.zeros_like(pieces_ref)
    count = 0
    for column in range(4 * channels // 128):
        part = grad_ref[:, column * 128 : (column + 1) * 128].astype(bf16)
        pieces_ref[count : count + channels // ROWS] = part.reshape(channels // ROWS, ROWS, 128)
        count += channels // ROWS
    rows_t = binned.shape[0] // ROWS
    for side in range(2):
        part = binned[:, side * 128 : (side + 1) * 128].astype(bf16)
        pieces_ref[count : count + rows_t] = part.reshape(rows_t, ROWS, 128)
        count += rows_t
    gain_low = gain_grad.astype(bf16)
    pieces_ref[count, 0:1, :] = gain_low[:, :128]
    pieces_ref[count, 1:2, : channels - 128] = gain_low[:, 128:]


def finish_kernel(
    nlat, nlon, res_ref, own_ref, pieces_ref,
    both_ref, qkv_ref, proj_ref, table_ref, gain_ref,
    land_ref, rs1_ref, mid_ref, rs2_ref, ag2_ref, ag_ref, grad_ref,
    sends, recvs, lon_send, lon_recv, lat_send, lat_recv,
):
    lat = lax.axis_index("lat")
    lon = lax.axis_index("lon")
    chunk = mid_ref.shape[0]
    share = chunk // nlat
    last = own_ref.shape[1] - 1
    down, right = lax.rem(lat + 1, nlat), lax.rem(lon + 1, nlon)
    up, left = lax.rem(lat + nlat - 1, nlat), lax.rem(lon + nlon - 1, nlon)

    barrier = pltpu.get_barrier_semaphore()
    for step in range(1, nlon):
        who = (lat, lax.rem(lon + step, nlon))
        pl.semaphore_signal(barrier, inc=1, device_id=who, device_id_type=MESH)
    for step in range(1, nlat):
        who = (lax.rem(lat + step, nlat), lon)
        pl.semaphore_signal(barrier, inc=1, device_id=who, device_id_type=MESH)
    pl.semaphore_signal(barrier, inc=1, device_id=(up, left), device_id_type=MESH)
    pl.semaphore_wait(barrier, nlon + nlat - 1)

    def along_lon(src, dst, which, step):
        return pltpu.make_async_remote_copy(
            src_ref=src, dst_ref=dst, send_sem=lon_send.at[which], recv_sem=lon_recv.at[which],
            device_id=(lat, lax.rem(lon + step, nlon)), device_id_type=MESH,
        )

    def along_lat(src, dst, which, step):
        return pltpu.make_async_remote_copy(
            src_ref=src, dst_ref=dst, send_sem=lat_send.at[which], recv_sem=lat_recv.at[which],
            device_id=(lax.rem(lat + step, nlat), lon), device_id_type=MESH,
        )

    @pl.loop(1, nlon)
    def _(step):
        who = lax.rem(lon + step, nlon)
        along_lon(
            pieces_ref.at[pl.ds(who * chunk, chunk)],
            rs1_ref.at[pl.ds((step - 1) * chunk, chunk)], 0, step,
        ).start()

    top = pl.ds(0, HALF_LAT)
    bottom = pl.ds(HALF_LAT, HALF_LAT)
    moves = (
        (res_ref.at[top, pl.ds(0, last)], land_ref.at[top, pl.ds(1, last)], (down, lon)),
        (res_ref.at[top, pl.ds(last, 1)], land_ref.at[top, pl.ds(0, 1)], (down, right)),
        (res_ref.at[bottom, pl.ds(last, 1)], land_ref.at[bottom, pl.ds(0, 1)], (lat, right)),
    )
    copies = [
        pltpu.make_async_remote_copy(
            src_ref=src, dst_ref=dst, send_sem=sends.at[i], recv_sem=recvs.at[i],
            device_id=who, device_id_type=MESH,
        )
        for i, (src, dst, who) in enumerate(moves)
    ]
    for copy in copies:
        copy.start()

    own_part = own_ref[bottom, 1:].astype(f32) + res_ref[bottom, :last].astype(f32)
    both_ref[bottom, 1:] = own_part.astype(bf16)

    pltpu.make_async_copy(rs1_ref, rs1_ref, lon_recv.at[0]).wait()
    summed = pieces_ref[pl.ds(lon * chunk, chunk)].astype(f32)
    for step in range(nlon - 1):
        summed = summed + rs1_ref[step * chunk : (step + 1) * chunk].astype(f32)
    mid_ref[...] = summed.astype(bf16)

    @pl.loop(1, nlat)
    def _(step):
        who = lax.rem(lat + step, nlat)
        along_lat(
            mid_ref.at[pl.ds(who * share, share)],
            rs2_ref.at[pl.ds((step - 1) * share, share)], 0, step,
        ).start()

    pltpu.make_async_copy(rs2_ref, rs2_ref, lat_recv.at[0]).wait()
    total = mid_ref[pl.ds(lat * share, share)].astype(f32)
    for step in range(nlat - 1):
        total = total + rs2_ref[step * share : (step + 1) * share].astype(f32)
    ag2_ref[pl.ds(lat * share, share)] = total.astype(bf16)

    @pl.loop(1, nlat)
    def _(step):
        mine = ag2_ref.at[pl.ds(lat * share, share)]
        along_lat(mine, mine, 1, step).start()

    pltpu.make_async_copy(rs2_ref, rs2_ref, lat_recv.at[1]).wait()

    @pl.loop(1, nlon)
    def _(step):
        along_lon(ag2_ref, ag_ref.at[pl.ds(lon * chunk, chunk)], 1, step).start()

    ag_ref[pl.ds(lon * chunk, chunk)] = ag2_ref[...]

    for copy in copies:
        copy.wait()
    both_ref[top] = (own_ref[top].astype(f32) + land_ref[top].astype(f32)).astype(bf16)
    both_ref[bottom, 0:1] = (
        own_ref[bottom, 0:1].astype(f32) + land_ref[bottom, 0:1].astype(f32)
    ).astype(bf16)

    pltpu.make_async_copy(rs1_ref, rs1_ref, lon_recv.at[1]).wait()
    channels = gain_ref.shape[1]
    at = 0
    for column in range(4 * channels // 128):
        part = ag_ref[at : at + channels // ROWS].astype(f32)
        grad_ref[:, column * 128 : (column + 1) * 128] = part.reshape(channels, 128)
        at += channels // ROWS
    kinds, heads, extent = table_ref.shape
    rows_t = kinds * heads // ROWS
    sides = []
    for side in range(2):
        sides.append(ag_ref[at : at + rows_t].astype(f32).reshape(kinds * heads, 128))
        at += rows_t
    table = jnp.concatenate(sides, axis=1)
    gain_block = ag_ref[at].astype(f32)
    gain = jnp.concatenate([gain_block[0:1], gain_block[1:2, : channels - 128]], axis=1)

    def scale(value, entries):
        mean = jnp.sum(jnp.sum(value * value, axis=1, keepdims=True), axis=0, keepdims=True)
        return jnp.minimum(1.0, lax.rsqrt(mean * (1.0 / entries) + clip_eps))

    wide = grad_ref[:, : 3 * channels]
    qkv_ref[...] = wide * scale(wide, wide.size)
    proj = grad_ref[:, 3 * channels :]
    proj_ref[...] = proj * scale(proj, proj.size)
    lane = lax.broadcasted_iota(jnp.int32, table.shape, 1)
    table = jnp.where(lane < extent, table, 0.0)
    table = table * scale(table, kinds * heads * extent)
    for kind in range(kinds):
        table_ref[kind] = table[kind * heads : (kind + 1) * heads, :extent]
    gain_ref[...] = gain * scale(gain, channels)

    for which in range(2):
        pltpu.make_async_copy(rs1_ref, rs1_ref, lon_send.at[which]).wait()
        pltpu.make_async_copy(rs2_ref, rs2_ref, lat_send.at[which]).wait()


def on_device(nlat, nlon, state_grid, norm_gain, w_qkv, w_proj, bias_table, window_kind, cotangent):
    rows_dev, cols_dev, channels = state_grid.shape
    halves = cols_dev // HALF_LON
    windows = cols_dev // WIN_LON
    kinds, heads, extent = bias_table.shape
    devices = nlat * nlon
    joint = jnp.concatenate([state_grid, cotangent], axis=2)
    joint = joint.reshape(rows_dev, halves, HALF_LON, 2 * channels)
    joint = jnp.pad(joint, ((0, 0), (0, 0), (0, PAD - HALF_LON), (0, 0)))
    grid_shape = joint.shape

    block = pl.pallas_call(
        functools.partial(halo_kernel, nlat, nlon),
        name="halo",
        out_shape=jax.ShapeDtypeStruct(grid_shape, bf16),
        in_specs=[VM],
        out_specs=VM,
        scratch_shapes=[
            pltpu.SemaphoreType.DMA((3,)),
            pltpu.SemaphoreType.DMA((3,)),
            pltpu.SemaphoreType.DMA(()),
        ],
        compiler_params=pltpu.CompilerParams(collective_id=0, has_side_effects=True),
    )(joint)

    wide = 2 * PAD
    four = (WIN_LAT, windows, wide)
    total = WIN_LAT * windows * wide
    tokens = WIN_LAT * wide
    used = 4 * channels // 128 * (channels // ROWS) + 2 * (kinds * heads // ROWS) + 1
    share = -(-used // devices)
    res, pieces = pl.pallas_call(
        attend_kernel,
        name="attend",
        out_shape=(
            jax.ShapeDtypeStruct(four + (2 * channels,), bf16),
            jax.ShapeDtypeStruct((share * devices, ROWS, 128), bf16),
        ),
        in_specs=[pl.BlockSpec(memory_space=pltpu.SMEM)] + [VM] * 5,
        out_specs=(VM, VM),
        scratch_shapes=[
            pltpu.VMEM((total, channels), f32),
            pltpu.VMEM((total, 1), f32),
            pltpu.VMEM((total, channels), bf16),
            pltpu.VMEM(four + (3 * channels,), bf16),
            pltpu.VMEM(four + (channels,), bf16),
            pltpu.VMEM((total, channels), bf16),
            pltpu.VMEM(four + (channels,), bf16),
            pltpu.VMEM(four + (3 * channels,), bf16),
            pltpu.VMEM((tokens, 128), f32),
            pltpu.VMEM((128, tokens), bf16),
            pltpu.VMEM((kinds, heads, 256), f32),
            pltpu.VMEM((kinds, heads, PAD, 256), f32),
            pltpu.VMEM((channels, 4 * channels), f32),
        ],
    )(
        window_kind,
        block.reshape(four + (2 * channels,)),
        norm_gain.reshape(1, channels),
        w_qkv,
        w_proj,
        bias_table,
    )

    both, qkv_grad, proj_grad, table_grad, gain_grad = pl.pallas_call(
        functools.partial(finish_kernel, nlat, nlon),
        name="finish",
        out_shape=(
            jax.ShapeDtypeStruct(grid_shape, bf16),
            jax.ShapeDtypeStruct((channels, 3 * channels), f32),
            jax.ShapeDtypeStruct((channels, channels), f32),
            jax.ShapeDtypeStruct((kinds, heads, extent), f32),
            jax.ShapeDtypeStruct((1, channels), f32),
        ),
        in_specs=[VM] * 3,
        out_specs=(VM,) * 5,
        scratch_shapes=[
            pltpu.VMEM(grid_shape, bf16),
            pltpu.VMEM((share * nlat * (nlon - 1), ROWS, 128), bf16),
            pltpu.VMEM((share * nlat, ROWS, 128), bf16),
            pltpu.VMEM((share * (nlat - 1), ROWS, 128), bf16),
            pltpu.VMEM((share * nlat, ROWS, 128), bf16),
            pltpu.VMEM((share * devices, ROWS, 128), bf16),
            pltpu.VMEM((channels, 4 * channels), f32),
            pltpu.SemaphoreType.DMA((3,)),
            pltpu.SemaphoreType.DMA((3,)),
            pltpu.SemaphoreType.DMA((2,)),
            pltpu.SemaphoreType.DMA((2,)),
            pltpu.SemaphoreType.DMA((2,)),
            pltpu.SemaphoreType.DMA((2,)),
        ],
        compiler_params=pltpu.CompilerParams(collective_id=1, has_side_effects=True),
    )(res.reshape(grid_shape), joint, pieces)

    both = both[:, :, :HALF_LON].reshape(rows_dev, cols_dev, 2 * channels)
    return (
        both[:, :, :channels],
        both[:, :, channels:],
        qkv_grad,
        proj_grad,
        table_grad,
        gain_grad.reshape(channels),
    )


def solution(mesh):
    in_specs = (P("lat", "lon", None), P(), P(), P(), P(), P(), P("lat", "lon", None))
    out_specs = (P("lat", "lon", None), P("lat", "lon", None), P(), P(), P(), P())
    body = functools.partial(on_device, mesh.shape["lat"], mesh.shape["lon"])
    return jax.shard_map(body, mesh=mesh, in_specs=in_specs, out_specs=out_specs, check_vma=False)
```

```python
import functools

import jax
import jax.numpy as jnp
from jax import lax
from jax.experimental import pallas as pl
from jax.experimental.pallas import tpu as pltpu
from jax.sharding import PartitionSpec as P

HEADS = 6
WIN_LAT = 6
WIN_LON = 12
HALF_LAT = 3
HALF_LON = 6
PAD = 8
ROWS = 8
SPAN = 2 * WIN_LON - 1
TOP = (WIN_LAT - 1) * SPAN + WIN_LON - 1

norm_eps = 1e-05
clip_eps = 1e-06
masked_score = -1e30
f32 = jnp.float32
bf16 = jnp.bfloat16
MESH = pl.DeviceIdType.MESH
VM = pl.BlockSpec(memory_space=pltpu.VMEM)


def nt(a, b):
    return lax.dot_general(a, b, (((1,), (1,)), ((), ())), preferred_element_type=f32)


def tn(a, b):
    return lax.dot_general(a, b, (((0,), (0,)), ((), ())), preferred_element_type=f32)


def nn(a, b):
    return jnp.dot(a, b, preferred_element_type=f32)


def block_kernel(
    nlat, nlon, kinds_ref, own_ref, gain_ref, wqkv_ref, wproj_ref, bias_ref,
    both_ref, qkv_out, proj_out, table_out, gain_out,
    block_ref, res_ref, pieces_ref,
    unit_ref, inv_ref, normed_ref, qkv_ref, dmix_ref, g_ref, mixed_ref, dqkv_ref,
    neg_ref, emb_ref, table_in, table_ref, grad_ref,
    land_ref, rs1_ref, mid_ref, rs2_ref, ag2_ref, ag_ref,
    halo_send, halo_recv, local, sends, recvs, lon_send, lon_recv, lat_send, lat_recv,
):
    lat = lax.axis_index("lat")
    lon = lax.axis_index("lon")
    _, halves, _, twice = own_ref.shape
    channels = twice // 2
    windows = halves // 2
    wide = 2 * PAD
    last = halves - 1
    tokens = WIN_LAT * wide
    head = channels // HEADS
    inv_sqrt = head ** (-0.5)
    total = WIN_LAT * windows * wide
    four = (WIN_LAT, windows, wide)
    chunk = mid_ref.shape[0]
    share = chunk // nlat
    down, right = lax.rem(lat + 1, nlat), lax.rem(lon + 1, nlon)
    up, left = lax.rem(lat + nlat - 1, nlat), lax.rem(lon + nlon - 1, nlon)

    barrier = pltpu.get_barrier_semaphore()
    for step in range(1, nlon):
        who = (lat, lax.rem(lon + step, nlon))
        pl.semaphore_signal(barrier, inc=1, device_id=who, device_id_type=MESH)
    for step in range(1, nlat):
        who = (lax.rem(lat + step, nlat), lon)
        pl.semaphore_signal(barrier, inc=1, device_id=who, device_id_type=MESH)
    for who in ((up, left), (down, right)):
        pl.semaphore_signal(barrier, inc=1, device_id=who, device_id_type=MESH)
    pl.semaphore_wait(barrier, nlon + nlat)

    top = pl.ds(0, HALF_LAT)
    bottom = pl.ds(HALF_LAT, HALF_LAT)
    inner = pl.ds(1, last)
    moves = (
        (own_ref.at[bottom, pl.ds(0, 1)], block_ref.at[bottom, pl.ds(last, 1)], (lat, left)),
        (own_ref.at[top, inner], block_ref.at[top, pl.ds(0, last)], (up, lon)),
        (own_ref.at[top, pl.ds(0, 1)], block_ref.at[top, pl.ds(last, 1)], (up, left)),
    )
    fetch = [
        pltpu.make_async_remote_copy(
            src_ref=src, dst_ref=dst, send_sem=halo_send.at[i], recv_sem=halo_recv.at[i],
            device_id=who, device_id_type=MESH,
        )
        for i, (src, dst, who) in enumerate(moves)
    ]
    for copy in fetch:
        copy.start()
    keep = pltpu.make_async_copy(
        own_ref.at[bottom, inner], block_ref.at[bottom, pl.ds(0, last)], local
    )
    keep.start()

    def prepare(first):
        here = slice(first, first + HALF_LAT)
        count = HALF_LAT * windows * wide
        rows = slice(first * windows * wide, first * windows * wide + count)
        three = (HALF_LAT, windows, wide)
        x = block_ref[here, :, :, :channels].astype(f32).reshape(count, channels)
        g = block_ref[here, :, :, channels:].astype(f32).reshape(count, channels).astype(bf16)
        g_ref[rows] = g
        centre = x - jnp.mean(x, axis=-1, keepdims=True)
        inverse = lax.rsqrt(jnp.mean(centre * centre, axis=-1, keepdims=True) + norm_eps)
        unit = centre * inverse
        unit_ref[rows] = unit
        inv_ref[rows] = inverse
        normed = (unit * gain_ref[...]).astype(bf16)
        normed_ref[rows] = normed
        qkv_ref[here] = nn(normed, wqkv_ref[...]).astype(bf16).reshape(three + (3 * channels,))
        dmix_ref[here] = nt(g, wproj_ref[...]).astype(bf16).reshape(three + (channels,))

    def place(index):
        slot = index >> 4
        row = jnp.where(slot >= HALF_LAT, slot - HALF_LAT, slot + HALF_LAT)
        side = (index >> 3) & 1
        column = index & 7
        return row, column, SPAN * row + HALF_LON * side + column

    row_i, _, _ = place(lax.broadcasted_iota(jnp.int32, (tokens, 128), 0))
    lane = TOP - lax.broadcasted_iota(jnp.int32, (tokens, 128), 1)
    good = lane > TOP
    for row in range(WIN_LAT):
        start = SPAN * row
        fits = (lane >= start) & (lane < start + WIN_LON)
        same = (row_i < HALF_LAT) if row < HALF_LAT else (row_i >= HALF_LAT)
        good = good | (fits & (same | (lat < nlat - 1)))
    neg_ref[...] = jnp.where(good, 0.0, masked_score)
    slot_j, column_j, place_j = place(lax.broadcasted_iota(jnp.int32, (128, tokens), 1))
    spot = TOP - lax.broadcasted_iota(jnp.int32, (128, tokens), 0)
    emb_ref[...] = jnp.where((spot == place_j) & (column_j < HALF_LON), 1.0, 0.0).astype(bf16)

    table_in[...] = jnp.zeros_like(table_in)
    table_in[:, :, : bias_ref.shape[2]] = bias_ref[...]
    table_ref[...] = jnp.zeros_like(table_ref)

    keep.wait()
    fetch[0].wait_recv()
    prepare(HALF_LAT)
    fetch[1].wait_recv()
    fetch[2].wait_recv()
    prepare(0)

    lane8 = lax.broadcasted_iota(jnp.int32, (PAD, 128), 1)
    kind_of = lax.broadcasted_iota(jnp.int32, (bias_ref.shape[1], PAD, 256), 0)
    sub8 = lax.broadcasted_iota(jnp.int32, (PAD, 256), 0)
    head_of = lax.broadcasted_iota(jnp.int32, (1, channels), 1) // head
    masks = [(head_of == h).astype(bf16) for h in range(HEADS)]
    masks32 = [(head_of == h).astype(f32) for h in range(HEADS)]
    bases = []
    for block in range(tokens // PAD):
        slot, side = block // 2, block % 2
        bases.append(SPAN * ((slot + HALF_LAT) % WIN_LAT) + HALF_LON * side)

    @pl.loop(0, windows)
    def _(w):
        kind = kinds_ref[lat, lon * windows + w]
        qkv = qkv_ref[:, w].reshape(tokens, 3 * channels)
        queries = qkv[:, :channels]
        emb = emb_ref[...]
        kv = nn(emb, qkv[:, channels:]).astype(bf16)
        keys, values = kv[:, :channels], kv[:, channels:]
        dmix = dmix_ref[:, w].reshape(tokens, channels)
        q_all = jnp.concatenate([queries * m for m in masks], axis=0)
        d_all = jnp.concatenate([dmix * m for m in masks], axis=0)
        raw = nt(q_all, keys)
        parts = []
        for h in range(HEADS):
            base = jnp.broadcast_to(table_in[h, pl.ds(kind, 1)], (PAD, 256))
            for bit in (1, 2, 4):
                base = jnp.where((sub8 & bit) != 0, pltpu.roll(base, 256 - bit, 1), base)
            low, high = base[:, :128], base[:, 128:]
            for shift in bases:
                if shift == 0:
                    parts.append(low)
                else:
                    parts.append(
                        jnp.where(
                            lane8 < 128 - shift,
                            pltpu.roll(low, 128 - shift, 1),
                            pltpu.roll(high, 128 - shift, 1),
                        )
                    )
        bias = jnp.concatenate(parts, axis=0)
        neg = neg_ref[...]
        scores = raw * inv_sqrt + bias + jnp.concatenate([neg] * HEADS, axis=0)
        expo = jnp.exp(scores - jnp.max(scores, axis=-1, keepdims=True))
        probs = expo * (1.0 / jnp.sum(expo, axis=-1, keepdims=True))
        low_p = probs.astype(bf16)

        def fold(stacked):
            out = stacked[:tokens] * masks32[0]
            for h in range(1, HEADS):
                out = out + stacked[h * tokens : (h + 1) * tokens] * masks32[h]
            return out

        mixed_ref[:, w] = fold(nn(low_p, values)).astype(bf16).reshape(WIN_LAT, wide, channels)
        d_probs = nt(d_all, values)
        d_scores = probs * (d_probs - jnp.sum(probs * d_probs, axis=-1, keepdims=True))
        low_d = d_scores.astype(bf16)
        d_q = (fold(nn(low_d, keys)) * inv_sqrt).astype(bf16)
        d_k = (tn(low_d, q_all) * inv_sqrt).astype(bf16)
        d_v = tn(low_p, d_all).astype(bf16)
        d_kv = tn(emb, jnp.concatenate([d_k, d_v], axis=1)).astype(bf16)
        dqkv_ref[:, w] = jnp.concatenate([d_q, d_kv], axis=1).reshape(WIN_LAT, wide, 3 * channels)
        for h in range(HEADS):
            low = jnp.zeros((PAD, 128), f32)
            high = jnp.zeros((PAD, 128), f32)
            for block, shift in enumerate(bases):
                at = h * tokens + block * PAD
                tile = d_scores[at : at + PAD]
                if shift == 0:
                    low = low + tile
                else:
                    turned = pltpu.roll(tile, shift, 1)
                    low = low + jnp.where(lane8 >= shift, turned, 0.0)
                    high = high + jnp.where(lane8 < shift, turned, 0.0)
            tile = jnp.concatenate([low, high], axis=1)
            table_ref[h] += jnp.where(kind_of == kind, tile[None], 0.0)

    mixed = mixed_ref[...].reshape(total, channels)
    d_qkv = dqkv_ref[...].reshape(total, 3 * channels)
    branch = nn(mixed, wproj_ref[...])
    d_normed = nt(d_qkv, wqkv_ref[...])
    unit = unit_ref[...]
    d_unit = d_normed * gain_ref[...]
    path = inv_ref[...] * (
        d_unit
        - jnp.mean(d_unit, axis=-1, keepdims=True)
        - unit * jnp.mean(d_unit * unit, axis=-1, keepdims=True)
    )
    grid = (WIN_LAT, halves, PAD, channels)
    res_ref[:, :, :, :channels] = branch.reshape(grid).astype(bf16)
    res_ref[:, :, :, channels:] = path.reshape(grid).astype(bf16)
    gain_grad = jnp.sum(d_normed * unit, axis=0, keepdims=True)
    moves = (
        (res_ref.at[top, pl.ds(0, last)], land_ref.at[top, pl.ds(1, last)], (down, lon)),
        (res_ref.at[top, pl.ds(last, 1)], land_ref.at[top, pl.ds(0, 1)], (down, right)),
        (res_ref.at[bottom, pl.ds(last, 1)], land_ref.at[bottom, pl.ds(0, 1)], (lat, right)),
    )
    copies = [
        pltpu.make_async_remote_copy(
            src_ref=src, dst_ref=dst, send_sem=sends.at[i], recv_sem=recvs.at[i],
            device_id=who, device_id_type=MESH,
        )
        for i, (src, dst, who) in enumerate(moves)
    ]
    for copy in copies:
        copy.start()
    grad_ref[:, : 3 * channels] = tn(normed_ref[...], d_qkv)
    grad_ref[:, 3 * channels :] = tn(mixed, g_ref[...])

    table = table_ref[...]
    sub = lax.broadcasted_iota(jnp.int32, table.shape, 2)
    flat = table.reshape(-1, 256)
    sub = sub.reshape(-1, 256)
    for bit in (1, 2, 4):
        flat = jnp.where((sub & bit) != 0, pltpu.roll(flat, bit, 1), flat)
    binned = jnp.sum(flat.reshape(HEADS * table.shape[1], PAD, 256), axis=1)

    pieces_ref[...] = jnp.zeros_like(pieces_ref)
    count = 0
    for column in range(4 * channels // 128):
        part = grad_ref[:, column * 128 : (column + 1) * 128].astype(bf16)
        pieces_ref[count : count + channels // ROWS] = part.reshape(channels // ROWS, ROWS, 128)
        count += channels // ROWS
    rows_t = binned.shape[0] // ROWS
    for side in range(2):
        part = binned[:, side * 128 : (side + 1) * 128].astype(bf16)
        pieces_ref[count : count + rows_t] = part.reshape(rows_t, ROWS, 128)
        count += rows_t
    gain_low = gain_grad.astype(bf16)
    pieces_ref[count, 0:1, :] = gain_low[:, :128]
    pieces_ref[count, 1:2, : channels - 128] = gain_low[:, 128:]

    def along_lon(src, dst, which, step):
        return pltpu.make_async_remote_copy(
            src_ref=src, dst_ref=dst, send_sem=lon_send.at[which], recv_sem=lon_recv.at[which],
            device_id=(lat, lax.rem(lon + step, nlon)), device_id_type=MESH,
        )

    def along_lat(src, dst, which, step):
        return pltpu.make_async_remote_copy(
            src_ref=src, dst_ref=dst, send_sem=lat_send.at[which], recv_sem=lat_recv.at[which],
            device_id=(lax.rem(lat + step, nlat), lon), device_id_type=MESH,
        )

    @pl.loop(1, nlon)
    def _(step):
        who = lax.rem(lon + step, nlon)
        along_lon(
            pieces_ref.at[pl.ds(who * chunk, chunk)],
            rs1_ref.at[pl.ds((step - 1) * chunk, chunk)], 0, step,
        ).start()

    own_part = own_ref[bottom, 1:].astype(f32) + res_ref[bottom, :last].astype(f32)
    both_ref[bottom, 1:] = own_part.astype(bf16)

    pltpu.make_async_copy(rs1_ref, rs1_ref, lon_recv.at[0]).wait()
    summed = pieces_ref[pl.ds(lon * chunk, chunk)].astype(f32)
    for step in range(nlon - 1):
        summed = summed + rs1_ref[step * chunk : (step + 1) * chunk].astype(f32)
    mid_ref[...] = summed.astype(bf16)

    @pl.loop(1, nlat)
    def _(step):
        who = lax.rem(lat + step, nlat)
        along_lat(
            mid_ref.at[pl.ds(who * share, share)],
            rs2_ref.at[pl.ds((step - 1) * share, share)], 0, step,
        ).start()

    pltpu.make_async_copy(rs2_ref, rs2_ref, lat_recv.at[0]).wait()
    final = mid_ref[pl.ds(lat * share, share)].astype(f32)
    for step in range(nlat - 1):
        final = final + rs2_ref[step * share : (step + 1) * share].astype(f32)
    ag2_ref[pl.ds(lat * share, share)] = final.astype(bf16)

    @pl.loop(1, nlat)
    def _(step):
        mine = ag2_ref.at[pl.ds(lat * share, share)]
        along_lat(mine, mine, 1, step).start()

    pltpu.make_async_copy(rs2_ref, rs2_ref, lat_recv.at[1]).wait()

    @pl.loop(1, nlon)
    def _(step):
        along_lon(ag2_ref, ag_ref.at[pl.ds(lon * chunk, chunk)], 1, step).start()

    ag_ref[pl.ds(lon * chunk, chunk)] = ag2_ref[...]

    for copy in copies:
        copy.wait()
    both_ref[top] = (own_ref[top].astype(f32) + land_ref[top].astype(f32)).astype(bf16)
    both_ref[bottom, 0:1] = (
        own_ref[bottom, 0:1].astype(f32) + land_ref[bottom, 0:1].astype(f32)
    ).astype(bf16)

    pltpu.make_async_copy(rs1_ref, rs1_ref, lon_recv.at[1]).wait()
    at = 0
    for column in range(4 * channels // 128):
        part = ag_ref[at : at + channels // ROWS].astype(f32)
        grad_ref[:, column * 128 : (column + 1) * 128] = part.reshape(channels, 128)
        at += channels // ROWS
    heads, kinds, extent = table_out.shape
    rows_t = kinds * heads // ROWS
    sides = []
    for side in range(2):
        sides.append(ag_ref[at : at + rows_t].astype(f32).reshape(kinds * heads, 128))
        at += rows_t
    table = jnp.concatenate(sides, axis=1)
    gain_block = ag_ref[at].astype(f32)
    gain = jnp.concatenate([gain_block[0:1], gain_block[1:2, : channels - 128]], axis=1)

    def scale(value, entries):
        mean = jnp.sum(jnp.sum(value * value, axis=1, keepdims=True), axis=0, keepdims=True)
        return jnp.minimum(1.0, lax.rsqrt(mean * (1.0 / entries) + clip_eps))

    big = grad_ref[:, : 3 * channels]
    qkv_out[...] = big * scale(big, big.size)
    proj = grad_ref[:, 3 * channels :]
    proj_out[...] = proj * scale(proj, proj.size)
    lane = lax.broadcasted_iota(jnp.int32, table.shape, 1)
    table = jnp.where(lane < extent, table, 0.0)
    table = table * scale(table, kinds * heads * extent)
    for h in range(heads):
        table_out[h] = table[h * kinds : (h + 1) * kinds, :extent]
    gain_out[...] = gain * scale(gain, channels)

    for which in range(2):
        pltpu.make_async_copy(rs1_ref, rs1_ref, lon_send.at[which]).wait()
        pltpu.make_async_copy(rs2_ref, rs2_ref, lat_send.at[which]).wait()
    for copy in fetch:
        copy.wait_send()


def on_device(nlat, nlon, state_grid, norm_gain, w_qkv, w_proj, bias_table, window_kind, cotangent):
    rows_dev, cols_dev, channels = state_grid.shape
    halves = cols_dev // HALF_LON
    windows = cols_dev // WIN_LON
    kinds, heads, extent = bias_table.shape
    devices = nlat * nlon
    joint = jnp.concatenate([state_grid, cotangent], axis=2)
    joint = joint.reshape(rows_dev, halves, HALF_LON, 2 * channels)
    joint = jnp.pad(joint, ((0, 0), (0, 0), (0, PAD - HALF_LON), (0, 0)))
    grid_shape = joint.shape

    wide = 2 * PAD
    four = (WIN_LAT, windows, wide)
    total = WIN_LAT * windows * wide
    tokens = WIN_LAT * wide
    used = 4 * channels // 128 * (channels // ROWS) + 2 * (kinds * heads // ROWS) + 1
    share = -(-used // devices)
    both, qkv_grad, proj_grad, table_grad, gain_grad = pl.pallas_call(
        functools.partial(block_kernel, nlat, nlon),
        name="block",
        out_shape=(
            jax.ShapeDtypeStruct(grid_shape, bf16),
            jax.ShapeDtypeStruct((channels, 3 * channels), f32),
            jax.ShapeDtypeStruct((channels, channels), f32),
            jax.ShapeDtypeStruct((heads, kinds, extent), f32),
            jax.ShapeDtypeStruct((1, channels), f32),
        ),
        in_specs=[pl.BlockSpec(memory_space=pltpu.SMEM)] + [VM] * 5,
        out_specs=(VM,) * 5,
        scratch_shapes=[
            pltpu.VMEM(grid_shape, bf16),
            pltpu.VMEM(grid_shape, bf16),
            pltpu.VMEM((share * devices, ROWS, 128), bf16),
            pltpu.VMEM((total, channels), f32),
            pltpu.VMEM((total, 1), f32),
            pltpu.VMEM((total, channels), bf16),
            pltpu.VMEM(four + (3 * channels,), bf16),
            pltpu.VMEM(four + (channels,), bf16),
            pltpu.VMEM((total, channels), bf16),
            pltpu.VMEM(four + (channels,), bf16),
            pltpu.VMEM(four + (3 * channels,), bf16),
            pltpu.VMEM((tokens, 128), f32),
            pltpu.VMEM((128, tokens), bf16),
            pltpu.VMEM((heads, kinds, 256), f32),
            pltpu.VMEM((heads, kinds, PAD, 256), f32),
            pltpu.VMEM((channels, 4 * channels), f32),
            pltpu.VMEM(grid_shape, bf16),
            pltpu.VMEM((share * nlat * (nlon - 1), ROWS, 128), bf16),
            pltpu.VMEM((share * nlat, ROWS, 128), bf16),
            pltpu.VMEM((share * (nlat - 1), ROWS, 128), bf16),
            pltpu.VMEM((share * nlat, ROWS, 128), bf16),
            pltpu.VMEM((share * devices, ROWS, 128), bf16),
            pltpu.SemaphoreType.DMA((3,)),
            pltpu.SemaphoreType.DMA((3,)),
            pltpu.SemaphoreType.DMA(()),
            pltpu.SemaphoreType.DMA((3,)),
            pltpu.SemaphoreType.DMA((3,)),
            pltpu.SemaphoreType.DMA((2,)),
            pltpu.SemaphoreType.DMA((2,)),
            pltpu.SemaphoreType.DMA((2,)),
            pltpu.SemaphoreType.DMA((2,)),
        ],
        compiler_params=pltpu.CompilerParams(collective_id=0, has_side_effects=True),
    )(
        window_kind,
        joint,
        norm_gain.reshape(1, channels),
        w_qkv,
        w_proj,
        bias_table.transpose(1, 0, 2),
    )

    both = both[:, :, :HALF_LON].reshape(rows_dev, cols_dev, 2 * channels)
    return (
        both[:, :, :channels],
        both[:, :, channels:],
        qkv_grad,
        proj_grad,
        table_grad.transpose(1, 0, 2),
        gain_grad.reshape(channels),
    )


def solution(mesh):
    in_specs = (P("lat", "lon", None), P(), P(), P(), P(), P(), P("lat", "lon", None))
    out_specs = (P("lat", "lon", None), P("lat", "lon", None), P(), P(), P(), P())
    body = functools.partial(on_device, mesh.shape["lat"], mesh.shape["lon"])
    return jax.shard_map(body, mesh=mesh, in_specs=in_specs, out_specs=out_specs, check_vma=False)
```

```python
import functools

import jax
import jax.numpy as jnp
from jax import lax
from jax.experimental import pallas as pl
from jax.experimental.pallas import tpu as pltpu
from jax.sharding import PartitionSpec as P

HEADS = 6
WIN_LAT = 6
WIN_LON = 12
HALF_LAT = 3
HALF_LON = 6
PAD = 8
ROWS = 8
SPAN = 2 * WIN_LON - 1
TOP = (WIN_LAT - 1) * SPAN + WIN_LON - 1

norm_eps = 1e-05
clip_eps = 1e-06
masked_score = -1e30
f32 = jnp.float32
bf16 = jnp.bfloat16
MESH = pl.DeviceIdType.MESH
VM = pl.BlockSpec(memory_space=pltpu.VMEM)


def nt(a, b):
    return lax.dot_general(a, b, (((1,), (1,)), ((), ())), preferred_element_type=f32)


def tn(a, b):
    return lax.dot_general(a, b, (((0,), (0,)), ((), ())), preferred_element_type=f32)


def nn(a, b):
    return jnp.dot(a, b, preferred_element_type=f32)


def block_kernel(
    nlat, nlon, kinds_ref, own_ref, gain_ref, wqkv_ref, wproj_ref, bias_ref,
    both_ref, qkv_out, proj_out, table_out, gain_out,
    block_ref, res_ref, pieces_ref,
    unit_ref, inv_ref, normed_ref, qkv_ref, dmix_ref, g_ref, mixed_ref, dqkv_ref,
    neg_ref, emb_ref, table_in, table_ref, grad_ref,
    land_ref, rs1_ref, mid_ref, rs2_ref, ag2_ref, ag_ref,
    halo_send, halo_recv, row_send, row_recv, local, sends, recvs, lon_send, lon_recv, lat_send, lat_recv,
):
    lat = lax.axis_index("lat")
    lon = lax.axis_index("lon")
    _, halves, _, twice = own_ref.shape
    channels = twice // 2
    windows = halves // 2
    wide = 2 * PAD
    last = halves - 1
    tokens = WIN_LAT * wide
    head = channels // HEADS
    inv_sqrt = head ** (-0.5)
    total = WIN_LAT * windows * wide
    four = (WIN_LAT, windows, wide)
    chunk = mid_ref.shape[0]
    share = chunk // nlat
    down, right = lax.rem(lat + 1, nlat), lax.rem(lon + 1, nlon)
    up, left = lax.rem(lat + nlat - 1, nlat), lax.rem(lon + nlon - 1, nlon)

    barrier = pltpu.get_barrier_semaphore()
    for step in range(1, nlon):
        who = (lat, lax.rem(lon + step, nlon))
        pl.semaphore_signal(barrier, inc=1, device_id=who, device_id_type=MESH)
    for step in range(1, nlat):
        who = (lax.rem(lat + step, nlat), lon)
        pl.semaphore_signal(barrier, inc=1, device_id=who, device_id_type=MESH)
    for who in ((up, left), (down, right)):
        pl.semaphore_signal(barrier, inc=1, device_id=who, device_id_type=MESH)
    pl.semaphore_wait(barrier, nlon + nlat)

    top = pl.ds(0, HALF_LAT)
    bottom = pl.ds(HALF_LAT, HALF_LAT)
    inner = pl.ds(1, last)
    moves = (
        (own_ref.at[bottom, pl.ds(0, 1)], block_ref.at[bottom, pl.ds(last, 1)], (lat, left)),
        (own_ref.at[top, pl.ds(0, 1)], block_ref.at[top, pl.ds(last, 1)], (up, left)),
        (own_ref.at[top, pl.ds(last, 1)], block_ref.at[top, pl.ds(last - 1, 1)], (up, lon)),
    )
    fetch = [
        pltpu.make_async_remote_copy(
            src_ref=src, dst_ref=dst, send_sem=halo_send.at[i], recv_sem=halo_recv.at[i],
            device_id=who, device_id_type=MESH,
        )
        for i, (src, dst, who) in enumerate(moves)
    ]

    def fetch_rows(w):
        return pltpu.make_async_remote_copy(
            src_ref=own_ref.at[top, pl.ds(2 * w + 1, 2)],
            dst_ref=block_ref.at[top, pl.ds(2 * w, 2)],
            send_sem=row_send.at[w], recv_sem=row_recv.at[w],
            device_id=(up, lon), device_id_type=MESH,
        )

    for copy in fetch:
        copy.start()

    @pl.loop(0, windows - 1)
    def _(w):
        fetch_rows(w).start()

    keep = pltpu.make_async_copy(
        own_ref.at[bottom, inner], block_ref.at[bottom, pl.ds(0, last)], local
    )
    keep.start()

    def prepare(first):
        here = slice(first, first + HALF_LAT)
        count = HALF_LAT * windows * wide
        three = (HALF_LAT, windows, wide)
        x = block_ref[here, :, :, :channels].astype(f32).reshape(count, channels)
        g = block_ref[here, :, :, channels:].astype(f32).reshape(count, channels).astype(bf16)
        g_ref[here] = g.reshape(three + (channels,))
        centre = x - jnp.mean(x, axis=-1, keepdims=True)
        inverse = lax.rsqrt(jnp.mean(centre * centre, axis=-1, keepdims=True) + norm_eps)
        unit = centre * inverse
        unit_ref[here] = unit.reshape(three + (channels,))
        inv_ref[here] = inverse.reshape(three + (1,))
        normed = (unit * gain_ref[...]).astype(bf16)
        normed_ref[here] = normed.reshape(three + (channels,))
        qkv_ref[here] = nn(normed, wqkv_ref[...]).astype(bf16).reshape(three + (3 * channels,))
        dmix_ref[here] = nt(g, wproj_ref[...]).astype(bf16).reshape(three + (channels,))

    def prepare_window(w):
        here = slice(0, HALF_LAT)
        count = HALF_LAT * wide
        three = (HALF_LAT, wide)
        pair = pl.ds(2 * w, 2)
        x = block_ref[here, pair, :, :channels].astype(f32).reshape(count, channels)
        g = block_ref[here, pair, :, channels:].astype(f32).reshape(count, channels).astype(bf16)
        g_ref[here, w] = g.reshape(three + (channels,))
        centre = x - jnp.mean(x, axis=-1, keepdims=True)
        inverse = lax.rsqrt(jnp.mean(centre * centre, axis=-1, keepdims=True) + norm_eps)
        unit = centre * inverse
        unit_ref[here, w] = unit.reshape(three + (channels,))
        inv_ref[here, w] = inverse.reshape(three + (1,))
        normed = (unit * gain_ref[...]).astype(bf16)
        normed_ref[here, w] = normed.reshape(three + (channels,))
        qkv_ref[here, w] = nn(normed, wqkv_ref[...]).astype(bf16).reshape(three + (3 * channels,))
        dmix_ref[here, w] = nt(g, wproj_ref[...]).astype(bf16).reshape(three + (channels,))

    def place(index):
        slot = index >> 4
        row = jnp.where(slot >= HALF_LAT, slot - HALF_LAT, slot + HALF_LAT)
        side = (index >> 3) & 1
        column = index & 7
        return row, column, SPAN * row + HALF_LON * side + column

    row_i, _, _ = place(lax.broadcasted_iota(jnp.int32, (tokens, 128), 0))
    lane = TOP - lax.broadcasted_iota(jnp.int32, (tokens, 128), 1)
    good = lane > TOP
    for row in range(WIN_LAT):
        start = SPAN * row
        fits = (lane >= start) & (lane < start + WIN_LON)
        same = (row_i < HALF_LAT) if row < HALF_LAT else (row_i >= HALF_LAT)
        good = good | (fits & (same | (lat < nlat - 1)))
    neg_ref[...] = jnp.where(good, 0.0, masked_score)
    slot_j, column_j, place_j = place(lax.broadcasted_iota(jnp.int32, (128, tokens), 1))
    spot = TOP - lax.broadcasted_iota(jnp.int32, (128, tokens), 0)
    emb_ref[...] = jnp.where((spot == place_j) & (column_j < HALF_LON), 1.0, 0.0).astype(bf16)

    table_in[...] = jnp.zeros_like(table_in)
    table_in[:, :, : bias_ref.shape[2]] = bias_ref[...]
    table_ref[...] = jnp.zeros_like(table_ref)

    keep.wait()
    fetch[0].wait_recv()
    prepare(HALF_LAT)
    fetch[1].wait_recv()
    fetch[2].wait_recv()

    lane8 = lax.broadcasted_iota(jnp.int32, (PAD, 128), 1)
    kind_of = lax.broadcasted_iota(jnp.int32, (bias_ref.shape[1], PAD, 256), 0)
    sub8 = lax.broadcasted_iota(jnp.int32, (PAD, 256), 0)
    head_of = lax.broadcasted_iota(jnp.int32, (1, channels), 1) // head
    masks = [(head_of == h).astype(bf16) for h in range(HEADS)]
    masks32 = [(head_of == h).astype(f32) for h in range(HEADS)]
    bases = []
    for block in range(tokens // PAD):
        slot, side = block // 2, block % 2
        bases.append(SPAN * ((slot + HALF_LAT) % WIN_LAT) + HALF_LON * side)

    @pl.loop(0, windows)
    def _(w):
        @pl.when(w < windows - 1)
        def _():
            fetch_rows(w).wait_recv()

        prepare_window(w)
        kind = kinds_ref[lat, lon * windows + w]
        qkv = qkv_ref[:, w].reshape(tokens, 3 * channels)
        queries = qkv[:, :channels]
        emb = emb_ref[...]
        kv = nn(emb, qkv[:, channels:]).astype(bf16)
        keys, values = kv[:, :channels], kv[:, channels:]
        dmix = dmix_ref[:, w].reshape(tokens, channels)
        q_all = jnp.concatenate([queries * m for m in masks], axis=0)
        d_all = jnp.concatenate([dmix * m for m in masks], axis=0)
        raw = nt(q_all, keys)
        parts = []
        for h in range(HEADS):
            base = jnp.broadcast_to(table_in[h, pl.ds(kind, 1)], (PAD, 256))
            for bit in (1, 2, 4):
                base = jnp.where((sub8 & bit) != 0, pltpu.roll(base, 256 - bit, 1), base)
            low, high = base[:, :128], base[:, 128:]
            for shift in bases:
                if shift == 0:
                    parts.append(low)
                else:
                    parts.append(
                        jnp.where(
                            lane8 < 128 - shift,
                            pltpu.roll(low, 128 - shift, 1),
                            pltpu.roll(high, 128 - shift, 1),
                        )
                    )
        bias = jnp.concatenate(parts, axis=0)
        neg = neg_ref[...]
        scores = raw * inv_sqrt + bias + jnp.concatenate([neg] * HEADS, axis=0)
        expo = jnp.exp(scores - jnp.max(scores, axis=-1, keepdims=True))
        probs = expo * (1.0 / jnp.sum(expo, axis=-1, keepdims=True))
        low_p = probs.astype(bf16)

        def fold(stacked):
            out = stacked[:tokens] * masks32[0]
            for h in range(1, HEADS):
                out = out + stacked[h * tokens : (h + 1) * tokens] * masks32[h]
            return out

        mixed_ref[:, w] = fold(nn(low_p, values)).astype(bf16).reshape(WIN_LAT, wide, channels)
        d_probs = nt(d_all, values)
        d_scores = probs * (d_probs - jnp.sum(probs * d_probs, axis=-1, keepdims=True))
        low_d = d_scores.astype(bf16)
        d_q = (fold(nn(low_d, keys)) * inv_sqrt).astype(bf16)
        d_k = (tn(low_d, q_all) * inv_sqrt).astype(bf16)
        d_v = tn(low_p, d_all).astype(bf16)
        d_kv = tn(emb, jnp.concatenate([d_k, d_v], axis=1)).astype(bf16)
        dqkv_ref[:, w] = jnp.concatenate([d_q, d_kv], axis=1).reshape(WIN_LAT, wide, 3 * channels)
        for h in range(HEADS):
            low = jnp.zeros((PAD, 128), f32)
            high = jnp.zeros((PAD, 128), f32)
            for block, shift in enumerate(bases):
                at = h * tokens + block * PAD
                tile = d_scores[at : at + PAD]
                if shift == 0:
                    low = low + tile
                else:
                    turned = pltpu.roll(tile, shift, 1)
                    low = low + jnp.where(lane8 >= shift, turned, 0.0)
                    high = high + jnp.where(lane8 < shift, turned, 0.0)
            tile = jnp.concatenate([low, high], axis=1)
            table_ref[h] += jnp.where(kind_of == kind, tile[None], 0.0)

    mixed = mixed_ref[...].reshape(total, channels)
    d_qkv = dqkv_ref[...].reshape(total, 3 * channels)
    branch = nn(mixed, wproj_ref[...])
    d_normed = nt(d_qkv, wqkv_ref[...])
    unit = unit_ref[...].reshape(total, channels)
    d_unit = d_normed * gain_ref[...]
    path = inv_ref[...].reshape(total, 1) * (
        d_unit
        - jnp.mean(d_unit, axis=-1, keepdims=True)
        - unit * jnp.mean(d_unit * unit, axis=-1, keepdims=True)
    )
    grid = (WIN_LAT, halves, PAD, channels)
    res_ref[:, :, :, :channels] = branch.reshape(grid).astype(bf16)
    res_ref[:, :, :, channels:] = path.reshape(grid).astype(bf16)
    gain_grad = jnp.sum(d_normed * unit, axis=0, keepdims=True)
    moves = (
        (res_ref.at[top, pl.ds(0, last)], land_ref.at[top, pl.ds(1, last)], (down, lon)),
        (res_ref.at[top, pl.ds(last, 1)], land_ref.at[top, pl.ds(0, 1)], (down, right)),
        (res_ref.at[bottom, pl.ds(last, 1)], land_ref.at[bottom, pl.ds(0, 1)], (lat, right)),
    )
    copies = [
        pltpu.make_async_remote_copy(
            src_ref=src, dst_ref=dst, send_sem=sends.at[i], recv_sem=recvs.at[i],
            device_id=who, device_id_type=MESH,
        )
        for i, (src, dst, who) in enumerate(moves)
    ]
    for copy in copies:
        copy.start()
    grad_ref[:, : 3 * channels] = tn(normed_ref[...].reshape(total, channels), d_qkv)
    grad_ref[:, 3 * channels :] = tn(mixed, g_ref[...].reshape(total, channels))

    table = table_ref[...]
    sub = lax.broadcasted_iota(jnp.int32, table.shape, 2)
    flat = table.reshape(-1, 256)
    sub = sub.reshape(-1, 256)
    for bit in (1, 2, 4):
        flat = jnp.where((sub & bit) != 0, pltpu.roll(flat, bit, 1), flat)
    binned = jnp.sum(flat.reshape(HEADS * table.shape[1], PAD, 256), axis=1)

    pieces_ref[...] = jnp.zeros_like(pieces_ref)
    count = 0
    for column in range(4 * channels // 128):
        part = grad_ref[:, column * 128 : (column + 1) * 128].astype(bf16)
        pieces_ref[count : count + channels // ROWS] = part.reshape(channels // ROWS, ROWS, 128)
        count += channels // ROWS
    rows_t = binned.shape[0] // ROWS
    for side in range(2):
        part = binned[:, side * 128 : (side + 1) * 128].astype(bf16)
        pieces_ref[count : count + rows_t] = part.reshape(rows_t, ROWS, 128)
        count += rows_t
    gain_low = gain_grad.astype(bf16)
    pieces_ref[count, 0:1, :] = gain_low[:, :128]
    pieces_ref[count, 1:2, : channels - 128] = gain_low[:, 128:]

    def along_lon(src, dst, which, step):
        return pltpu.make_async_remote_copy(
            src_ref=src, dst_ref=dst, send_sem=lon_send.at[which], recv_sem=lon_recv.at[which],
            device_id=(lat, lax.rem(lon + step, nlon)), device_id_type=MESH,
        )

    def along_lat(src, dst, which, step):
        return pltpu.make_async_remote_copy(
            src_ref=src, dst_ref=dst, send_sem=lat_send.at[which], recv_sem=lat_recv.at[which],
            device_id=(lax.rem(lat + step, nlat), lon), device_id_type=MESH,
        )

    @pl.loop(1, nlon)
    def _(step):
        who = lax.rem(lon + step, nlon)
        along_lon(
            pieces_ref.at[pl.ds(who * chunk, chunk)],
            rs1_ref.at[pl.ds((step - 1) * chunk, chunk)], 0, step,
        ).start()

    own_part = own_ref[bottom, 1:].astype(f32) + res_ref[bottom, :last].astype(f32)
    both_ref[bottom, 1:] = own_part.astype(bf16)

    pltpu.make_async_copy(rs1_ref, rs1_ref, lon_recv.at[0]).wait()
    summed = pieces_ref[pl.ds(lon * chunk, chunk)].astype(f32)
    for step in range(nlon - 1):
        summed = summed + rs1_ref[step * chunk : (step + 1) * chunk].astype(f32)
    mid_ref[...] = summed.astype(bf16)

    @pl.loop(1, nlat)
    def _(step):
        who = lax.rem(lat + step, nlat)
        along_lat(
            mid_ref.at[pl.ds(who * share, share)],
            rs2_ref.at[pl.ds((step - 1) * share, share)], 0, step,
        ).start()

    pltpu.make_async_copy(rs2_ref, rs2_ref, lat_recv.at[0]).wait()
    final = mid_ref[pl.ds(lat * share, share)].astype(f32)
    for step in range(nlat - 1):
        final = final + rs2_ref[step * share : (step + 1) * share].astype(f32)
    ag2_ref[pl.ds(lat * share, share)] = final.astype(bf16)

    @pl.loop(1, nlat)
    def _(step):
        mine = ag2_ref.at[pl.ds(lat * share, share)]
        along_lat(mine, mine, 1, step).start()

    pltpu.make_async_copy(rs2_ref, rs2_ref, lat_recv.at[1]).wait()

    @pl.loop(1, nlon)
    def _(step):
        along_lon(ag2_ref, ag_ref.at[pl.ds(lon * chunk, chunk)], 1, step).start()

    ag_ref[pl.ds(lon * chunk, chunk)] = ag2_ref[...]

    for copy in copies:
        copy.wait()
    both_ref[top] = (own_ref[top].astype(f32) + land_ref[top].astype(f32)).astype(bf16)
    both_ref[bottom, 0:1] = (
        own_ref[bottom, 0:1].astype(f32) + land_ref[bottom, 0:1].astype(f32)
    ).astype(bf16)

    pltpu.make_async_copy(rs1_ref, rs1_ref, lon_recv.at[1]).wait()
    at = 0
    for column in range(4 * channels // 128):
        part = ag_ref[at : at + channels // ROWS].astype(f32)
        grad_ref[:, column * 128 : (column + 1) * 128] = part.reshape(channels, 128)
        at += channels // ROWS
    heads, kinds, extent = table_out.shape
    rows_t = kinds * heads // ROWS
    sides = []
    for side in range(2):
        sides.append(ag_ref[at : at + rows_t].astype(f32).reshape(kinds * heads, 128))
        at += rows_t
    table = jnp.concatenate(sides, axis=1)
    gain_block = ag_ref[at].astype(f32)
    gain = jnp.concatenate([gain_block[0:1], gain_block[1:2, : channels - 128]], axis=1)

    def scale(value, entries):
        mean = jnp.sum(jnp.sum(value * value, axis=1, keepdims=True), axis=0, keepdims=True)
        return jnp.minimum(1.0, lax.rsqrt(mean * (1.0 / entries) + clip_eps))

    big = grad_ref[:, : 3 * channels]
    qkv_out[...] = big * scale(big, big.size)
    proj = grad_ref[:, 3 * channels :]
    proj_out[...] = proj * scale(proj, proj.size)
    lane = lax.broadcasted_iota(jnp.int32, table.shape, 1)
    table = jnp.where(lane < extent, table, 0.0)
    table = table * scale(table, kinds * heads * extent)
    for h in range(heads):
        table_out[h] = table[h * kinds : (h + 1) * kinds, :extent]
    gain_out[...] = gain * scale(gain, channels)

    for which in range(2):
        pltpu.make_async_copy(rs1_ref, rs1_ref, lon_send.at[which]).wait()
        pltpu.make_async_copy(rs2_ref, rs2_ref, lat_send.at[which]).wait()
    for copy in fetch:
        copy.wait_send()

    @pl.loop(0, windows - 1)
    def _(w):
        fetch_rows(w).wait_send()


def on_device(nlat, nlon, state_grid, norm_gain, w_qkv, w_proj, bias_table, window_kind, cotangent):
    rows_dev, cols_dev, channels = state_grid.shape
    halves = cols_dev // HALF_LON
    windows = cols_dev // WIN_LON
    kinds, heads, extent = bias_table.shape
    devices = nlat * nlon
    joint = jnp.concatenate([state_grid, cotangent], axis=2)
    joint = joint.reshape(rows_dev, halves, HALF_LON, 2 * channels)
    joint = jnp.pad(joint, ((0, 0), (0, 0), (0, PAD - HALF_LON), (0, 0)))
    grid_shape = joint.shape

    wide = 2 * PAD
    four = (WIN_LAT, windows, wide)
    tokens = WIN_LAT * wide
    used = 4 * channels // 128 * (channels // ROWS) + 2 * (kinds * heads // ROWS) + 1
    share = -(-used // devices)
    both, qkv_grad, proj_grad, table_grad, gain_grad = pl.pallas_call(
        functools.partial(block_kernel, nlat, nlon),
        name="block",
        out_shape=(
            jax.ShapeDtypeStruct(grid_shape, bf16),
            jax.ShapeDtypeStruct((channels, 3 * channels), f32),
            jax.ShapeDtypeStruct((channels, channels), f32),
            jax.ShapeDtypeStruct((heads, kinds, extent), f32),
            jax.ShapeDtypeStruct((1, channels), f32),
        ),
        in_specs=[pl.BlockSpec(memory_space=pltpu.SMEM)] + [VM] * 5,
        out_specs=(VM,) * 5,
        scratch_shapes=[
            pltpu.VMEM(grid_shape, bf16),
            pltpu.VMEM(grid_shape, bf16),
            pltpu.VMEM((share * devices, ROWS, 128), bf16),
            pltpu.VMEM(four + (channels,), f32),
            pltpu.VMEM(four + (1,), f32),
            pltpu.VMEM(four + (channels,), bf16),
            pltpu.VMEM(four + (3 * channels,), bf16),
            pltpu.VMEM(four + (channels,), bf16),
            pltpu.VMEM(four + (channels,), bf16),
            pltpu.VMEM(four + (channels,), bf16),
            pltpu.VMEM(four + (3 * channels,), bf16),
            pltpu.VMEM((tokens, 128), f32),
            pltpu.VMEM((128, tokens), bf16),
            pltpu.VMEM((heads, kinds, 256), f32),
            pltpu.VMEM((heads, kinds, PAD, 256), f32),
            pltpu.VMEM((channels, 4 * channels), f32),
            pltpu.VMEM(grid_shape, bf16),
            pltpu.VMEM((share * nlat * (nlon - 1), ROWS, 128), bf16),
            pltpu.VMEM((share * nlat, ROWS, 128), bf16),
            pltpu.VMEM((share * (nlat - 1), ROWS, 128), bf16),
            pltpu.VMEM((share * nlat, ROWS, 128), bf16),
            pltpu.VMEM((share * devices, ROWS, 128), bf16),
            pltpu.SemaphoreType.DMA((3,)),
            pltpu.SemaphoreType.DMA((3,)),
            pltpu.SemaphoreType.DMA((windows - 1,)),
            pltpu.SemaphoreType.DMA((windows - 1,)),
            pltpu.SemaphoreType.DMA(()),
            pltpu.SemaphoreType.DMA((3,)),
            pltpu.SemaphoreType.DMA((3,)),
            pltpu.SemaphoreType.DMA((2,)),
            pltpu.SemaphoreType.DMA((2,)),
            pltpu.SemaphoreType.DMA((2,)),
            pltpu.SemaphoreType.DMA((2,)),
        ],
        compiler_params=pltpu.CompilerParams(collective_id=0, has_side_effects=True),
    )(
        window_kind,
        joint,
        norm_gain.reshape(1, channels),
        w_qkv,
        w_proj,
        bias_table.transpose(1, 0, 2),
    )

    both = both[:, :, :HALF_LON].reshape(rows_dev, cols_dev, 2 * channels)
    return (
        both[:, :, :channels],
        both[:, :, channels:],
        qkv_grad,
        proj_grad,
        table_grad.transpose(1, 0, 2),
        gain_grad.reshape(channels),
    )


def solution(mesh):
    in_specs = (P("lat", "lon", None), P(), P(), P(), P(), P(), P("lat", "lon", None))
    out_specs = (P("lat", "lon", None), P("lat", "lon", None), P(), P(), P(), P())
    body = functools.partial(on_device, mesh.shape["lat"], mesh.shape["lon"])
    return jax.shard_map(body, mesh=mesh, in_specs=in_specs, out_specs=out_specs, check_vma=False)
```
